32 devices in a mesh: region: 2 (over y), space: 8 (over z, x), day: 2 (over core).
Axes of the slice: x: 2, y: 2, z: 4, core: 2. Of those that a mesh axis runs over, the one named last changes fastest.
Arguments:
- observed: float32 [4, 64, 4096], P('day', ('region', 'space')), parts along dimension 1, may hold values from -20 to 20
- gap_mask: int32 [4, 64, 4096], P('day', ('region', 'space')), parts along dimension 1, may hold values 0 or 1
- sea_mask: int32 [64, 4096], P(('region', 'space')), parts along dimension 0, may hold values 0 or 1
- stencil: bfloat16 [9, 64, 4096], P(None, ('region', 'space')), parts along dimension 1, may hold values from 0.019897461 to 0.19921875
- precision: float32 [64, 4096], P(('region', 'space')), parts along dimension 0, may hold values from 0.5 to 4
- noise_precision: float32 [64, 4096], P(('region', 'space')), parts along dimension 0, may hold values from 0.5 to 8
- perturbation: bfloat16 [2, 4, 64, 4096], P(None, 'day', ('region', 'space')), parts along dimension 2, may hold values from -6 to 6
Outputs:
- posterior_mean: float32 [4, 64, 4096], P('day', ('region', 'space')), parts along dimension 1
- fitted: float32 [2, 64, 4096], P(None, ('region', 'space'), 'day'), parts along dimension 1
The draws below stay inside these ranges and needn't reach their ends.
There are 2 independent parts, one for each index of `region`. The reference program is written for one: setup_inputs(seed, part) draws one part's arguments, and reference() takes and returns one part's arrays. A program takes and returns all parts, laid end to end along the dimension named above; each array names one. Nothing has to cross between parts.
All inputs are finite; a program needn't handle non-finite values. No bound on the sum of `gap_mask` or of `sea_mask` on one device may be relied on, other than what follows from the above.
Results may differ from the reference program's by a relative error of at most 0.0003.
Values sent between devices are 32-bit elements; how exact they have to be, the bound alone decides.
No kernel may reach another device: no remote copies, remote signals or barrier semaphores. Data moves between devices by JAX's collectives and lax.ppermute only.
A program may use at most 64 MiB of HBM per device.

```python
import math
import jax
import jax.numpy as jnp
from jax import lax

COLS = 4096
ITERS = 2
ROWS = 32
DAYS = 4


def draw_observed(key, part):
    first_key, second_key = jax.random.split(key, 2)
    row_place = jnp.arange(ROWS, dtype=jnp.float32)[None, :, None] / ROWS
    column_draw = jax.random.uniform(first_key, (1, 1, COLS), jnp.float32)
    scale_field = 10.0 ** (0.6 * row_place + 0.4 * column_draw - 0.5)
    values = scale_field * jnp.clip(jax.random.normal(second_key, (DAYS, ROWS, COLS), jnp.float32), -6.0, 6.0)
    return values.astype(jnp.float32)


def set_ends(values, own_key, least, largest):
    index_at = [jax.random.randint(jax.random.fold_in(own_key, axis), (), 0, length) for axis, length in enumerate(values.shape)]
    longest = values.shape.index(max(values.shape))
    neighbour = index_at[:longest] + [(index_at[longest] + 1) % values.shape[longest]] + index_at[longest + 1:]
    return values.at[tuple(index_at)].set(least).at[tuple(neighbour)].set(largest)


def levels(stream_key, shape, shards, low, top_value):
    gain, own = 1.0, jax.random.fold_in(stream_key, 6)
    for axis_at, parts in shards:
        draws = jnp.exp(jax.random.uniform(jax.random.fold_in(own, axis_at), (parts,), jnp.float32, low / len(shards), top_value / len(shards)))
        gain = gain * jnp.repeat(draws, shape[axis_at] // parts).reshape([-1 if axis == axis_at else 1 for axis in range(len(shape))])
    return gain


def noise(rng, shape, scale, reach, shards=(), kind=jnp.bfloat16):
    loudness = levels(rng, shape, shards, -0.22, 0.18) if shards else 1.0
    drawn = jax.random.normal(rng, shape, jnp.float32) * scale * loudness
    return jnp.minimum(jnp.maximum(drawn, -reach), reach).astype(kind)


def setup_inputs(seed: int = 0, part: int = 0) -> dict:
    streams_of = jax.random.split(jax.random.key(seed), 8)
    own_keys = jax.random.split(jax.random.fold_in(streams_of[7], part), 8)
    return {
        "observed": draw_observed(jax.random.fold_in(jax.random.fold_in(streams_of[7], part), 71), part),
        "gap_mask": set_ends((jax.random.randint(own_keys[1], (DAYS, ROWS, COLS), 0, 4) < 3).astype(jnp.int32), jax.random.fold_in(own_keys[1], 1), 0, 1),
        "sea_mask": set_ends((jax.random.randint(own_keys[2], (ROWS, COLS), 0, 6) < 5).astype(jnp.int32), jax.random.fold_in(own_keys[2], 1), 0, 1),
        "stencil": jnp.clip(0.019897461 + 0.17932129 * jax.random.uniform(own_keys[3], (9, ROWS, COLS), jnp.float32) ** levels(own_keys[3], (9, ROWS, COLS), ((1, 8),), -0.2, 0.2), 0.019897461, 0.19921875).astype(jnp.bfloat16),
        "precision": jnp.clip(jnp.exp(math.log(4.0) - 2.0794415 * jax.random.uniform(own_keys[4], (ROWS, COLS), jnp.float32) ** levels(own_keys[4], (ROWS, COLS), ((0, 8),), -0.2, 0.2)), 0.5, 4.0),
        "noise_precision": jnp.clip(jnp.exp(math.log(8.0) - 2.7725887 * jax.random.uniform(own_keys[5], (ROWS, COLS), jnp.float32) ** levels(own_keys[5], (ROWS, COLS), ((0, 8),), -0.2, 0.2)), 0.5, 8.0),
        "perturbation": noise(own_keys[6], (2, DAYS, ROWS, COLS), 1.0, 6.0, ((1, 2), (2, 8))),
    }


OFFSETS = ((-1, -1), (-1, 0), (-1, 1), (0, -1), (0, 0), (0, 1), (1, -1), (1, 0), (1, 1))
RIDGE = 1.0

def displaced(values, row_step, col_step):
    height = values.shape[-2]
    breadth = values.shape[-1]
    padding = [(0, 0)] * (values.ndim - 2) + [(1, 1), (1, 1)]
    padded = jnp.pad(values, padding)
    return padded[..., 1 + row_step:1 + row_step + height, 1 + col_step:1 + col_step + breadth]

def forward(values, coefficients):
    result = jnp.zeros_like(values)
    for position, (row_step, col_step) in enumerate(OFFSETS):
        result = result + coefficients[position] * displaced(values, row_step, col_step)
    return result

def transposed(values, coefficients):
    result = jnp.zeros_like(values)
    for position, (row_step, col_step) in enumerate(OFFSETS):
        result = result + displaced(coefficients[position] * values, -row_step, -col_step)
    return result

def apply_precision(values, coefficients, precision, observed_precision, sea_float):
    masked = sea_float * values
    zero_plane = jnp.zeros_like(masked[:1])
    earlier = jnp.concatenate([zero_plane, masked[:-1]], 0)
    innovation = masked - forward(earlier, coefficients)
    weighted = precision * innovation
    following = jnp.concatenate([weighted[1:], zero_plane], 0)
    applied = weighted - transposed(following, coefficients) + observed_precision * masked
    return sea_float * applied + (1.0 - sea_float) * values

def conjugate_solve(right_side, coefficients, precision, observed_precision, sea_float):
    solution = jnp.zeros_like(right_side)
    residual = right_side
    direction = right_side
    norm_now = jnp.sum(residual * residual)
    for iteration in range(ITERS):
        applied = apply_precision(direction, coefficients, precision, observed_precision, sea_float)
        step_size = norm_now / jnp.sum(direction * applied)
        solution = solution + step_size * direction
        residual = residual - step_size * applied
        norm_next = jnp.sum(residual * residual)
        direction = residual + norm_next / norm_now * direction
        norm_now = norm_next
    return solution

def fit_cells(totals):
    diag_first = totals[0] + RIDGE
    cross_term = totals[1]
    diag_second = totals[2] + RIDGE
    determinant = diag_first * diag_second - cross_term * cross_term
    persistence = (diag_second * totals[3] - cross_term * totals[4]) / determinant
    diffusion = (diag_first * totals[4] - cross_term * totals[3]) / determinant
    return jnp.stack([persistence, diffusion], 0)

def reference(observed, gap_mask, sea_mask, stencil, precision, noise_precision, perturbation):
    sea_float = sea_mask.astype(jnp.float32)
    coefficients = stencil.astype(jnp.float32)
    observed_precision = noise_precision * gap_mask.astype(jnp.float32)
    base_side = sea_float * observed_precision * observed
    spread = sea_float * jnp.sqrt(precision + observed_precision)
    right_sides = [base_side, base_side + spread * perturbation[0].astype(jnp.float32), base_side + spread * perturbation[1].astype(jnp.float32)]
    solutions = [conjugate_solve(side, coefficients, precision, observed_precision, sea_float) for side in right_sides]
    samples = jnp.stack(solutions[1:], 0)
    centre = samples[:, :-1]
    target = samples[:, 1:]
    laplacian = -8.0 * centre
    for row_step, col_step in OFFSETS:
        if row_step != 0 or col_step != 0:
            laplacian = laplacian + displaced(centre, row_step, col_step)
    totals = jnp.stack([lax.optimization_barrier(jnp.sum(centre * centre, axis=(0, 1))), lax.optimization_barrier(jnp.sum(centre * laplacian, axis=(0, 1))), lax.optimization_barrier(jnp.sum(laplacian * laplacian, axis=(0, 1))), lax.optimization_barrier(jnp.sum(centre * target, axis=(0, 1))), lax.optimization_barrier(jnp.sum(laplacian * target, axis=(0, 1)))], 0)
    return (solutions[0], fit_cells(totals))
```

```python
import jax
import jax.numpy as jnp
from jax import lax
from jax.sharding import PartitionSpec as P

OFFSETS = ((-1, -1), (-1, 0), (-1, 1), (0, -1), (0, 0), (0, 1), (1, -1), (1, 0), (1, 1))
RIDGE = 1.0
LANES = 128


def send(x, space_of, day_of=lambda d: d):
    spaces, days = lax.axis_size("space"), lax.axis_size("day")
    pairs = []
    for s in range(spaces):
        for d in range(days):
            to_s, to_d = space_of(s), day_of(d)
            if 0 <= to_s < spaces:
                pairs.append((s * days + d, to_s * days + to_d))
    return lax.ppermute(x, ("space", "day"), pairs)


def column_shift(values, col_step):
    if col_step == 0:
        return values
    zero_column = jnp.zeros_like(values[..., :1])
    if col_step > 0:
        return jnp.concatenate([values[..., 1:], zero_column], -1)
    return jnp.concatenate([zero_column, values[..., :-1]], -1)


def forward(values, above, below, coefficients):
    rows = values.shape[-2]
    wide = jnp.concatenate([above[..., None, :], values, below[..., None, :]], -2)
    shifted = {c: column_shift(wide, c) for c in (-1, 0, 1)}
    total = 0.0
    for position, (a, c) in enumerate(OFFSETS):
        total = total + coefficients[position] * shifted[c][..., 1 + a : 1 + a + rows, :]
    return total


def transposed(values, coefficients):
    total = 0.0
    for c in (-1, 0, 1):
        part = 0.0
        for a in (-1, 0, 1):
            product = coefficients[3 * (a + 1) + c + 1] * values
            pad = [(0, 0)] * (values.ndim - 2) + [(1 + a, 1 - a), (0, 0)]
            part = part + jnp.pad(product, pad)
        total = total + column_shift(part, -c)
    return total


def fit_cells(totals):
    diag_first = totals[0] + RIDGE
    cross_term = totals[1]
    diag_second = totals[2] + RIDGE
    determinant = diag_first * diag_second - cross_term * cross_term
    persistence = (diag_second * totals[3] - cross_term * totals[4]) / determinant
    diffusion = (diag_first * totals[4] - cross_term * totals[3]) / determinant
    return jnp.stack([persistence, diffusion], 0)


def shards(observed, gap_mask, sea_mask, stencil, precision, noise_precision, perturbation):
    cols = observed.shape[-1]
    days = lax.axis_size("day")
    spaces = lax.axis_size("space")
    day = lax.axis_index("day")
    half = cols // days
    width = half + LANES
    start = day * (cols - width)
    other_start = (1 - day) * (cols - width)
    own = day * LANES

    def window(x, at=None):
        return lax.dynamic_slice_in_dim(x, start if at is None else at, width, x.ndim - 1)

    sea_all = sea_mask.astype(jnp.float32)
    obs_all = noise_precision * gap_mask.astype(jnp.float32)
    base = sea_all * obs_all * observed
    spread = sea_all * jnp.sqrt(precision + obs_all)
    fields = jnp.stack(
        [base, base + spread * perturbation[0].astype(jnp.float32), base + spread * perturbation[1].astype(jnp.float32), obs_all], 0
    )
    mine = window(fields)
    theirs = send(window(fields, other_start), lambda s: s, lambda d: 1 - d)
    is_first = day == 0
    both = jnp.concatenate([jnp.where(is_first, mine, theirs), jnp.where(is_first, theirs, mine)], 1)
    side, obs = both[:3], both[3]

    sea = window(sea_all)
    prec = window(precision)
    coefficients = window(stencil).astype(jnp.float32)

    def edge(row):
        return jnp.concatenate([side[:, :3, row].reshape(9, width), sea[row][None]], 0)

    above = send(edge(-1), lambda s: s + 1)
    below = send(edge(0), lambda s: s - 1)
    sea_above, sea_below = above[9], below[9]
    above, below = above[:9].reshape(3, 3, width), below[:9].reshape(3, 3, width)

    moved = forward(side[:, :3], above, below, coefficients)
    innovation = jnp.concatenate([side[:, :1], side[:, 1:] - moved], 1)
    weighted = prec * innovation
    scattered = transposed(weighted[:, 1:], coefficients)
    image = weighted + obs * side
    partial = sea * jnp.concatenate([image[:, :3] - scattered[:, :, 1:-1], image[:, 3:]], 1)

    to_above = jnp.stack([partial[:, :3, 0], scattered[:, :, 0]], 0).reshape(18, width)
    to_below = jnp.stack([partial[:, :3, -1], scattered[:, :, -1]], 0).reshape(18, width)
    from_above = send(to_below, lambda s: s + 1).reshape(2, 3, 3, width)
    from_below = send(to_above, lambda s: s - 1).reshape(2, 3, 3, width)
    fixed = jnp.concatenate(
        [
            partial[:, :3, :1] - sea[:1] * from_above[1][:, :, None],
            partial[:, :3, 1:-1],
            partial[:, :3, -1:] - sea[-1:] * from_below[1][:, :, None],
        ],
        2,
    )
    image = jnp.concatenate([fixed, partial[:, 3:]], 1)
    image_above = from_above[0] - sea_above * scattered[:, :, 0]
    image_below = from_below[0] - sea_below * scattered[:, :, -1]

    image_moved = forward(image[:, :3], image_above, image_below, coefficients)
    image_innovation = jnp.concatenate([image[:, :1], image[:, 1:] - image_moved], 1)

    def inner(x):
        return lax.dynamic_slice_in_dim(x, own, half, x.ndim - 1)

    b, z = inner(side), inner(image)

    def sums(x):
        return jnp.sum(x, axis=(1, 2, 3))

    energy = prec * image_innovation * image_innovation + obs * image * image
    scalars = jnp.stack([sums(b * b), sums(b * z), sums(z * z), sums(inner(energy))], 0)
    days_here = image.shape[1] // days
    image_swap = lax.dynamic_slice_in_dim(z[0], (1 - day) * days_here, days_here, 0)
    image_theirs = send(image_swap, lambda s: s, lambda d: 1 - d)

    if spaces & (spaces - 1) == 0:
        scalars = scalars + send(scalars, lambda s: s, lambda d: 1 - d)
        bit = 1
        while bit < spaces:
            scalars = scalars + send(scalars, lambda s: s ^ bit)
            bit *= 2
    else:
        scalars = lax.psum(scalars, ("space", "day"))
    m0, m1, m2, m3 = scalars
    first_step = m0 / m1
    norm_next = first_step * first_step * m2 - m0
    ratio = norm_next / m0
    grown = 1.0 + ratio
    curvature = grown * grown * m1 - 2.0 * first_step * grown * m2 + first_step * first_step * m3
    second_step = norm_next / curvature
    on_side = first_step + second_step * grown
    on_image = -second_step * first_step

    image_mine = lax.dynamic_slice_in_dim(z[0], day * days_here, days_here, 0)
    image_days = jnp.concatenate(
        [jnp.where(is_first, image_mine, image_theirs), jnp.where(is_first, image_theirs, image_mine)], -1
    )
    posterior = on_side[0] * base + on_image[0] * image_days

    def expand(v):
        return v[1:, None, None, None]

    wide_side = jnp.concatenate([above[1:, :, None], side[1:, :3], below[1:, :, None]], 2)
    wide_image = jnp.concatenate([image_above[1:, :, None], image[1:, :3], image_below[1:, :, None]], 2)
    earlier = expand(on_side) * wide_side + expand(on_image) * wide_image
    rows = side.shape[2]
    box = earlier[:, :, :rows] + earlier[:, :, 1 : 1 + rows] + earlier[:, :, 2:]
    centre = earlier[:, :, 1 : 1 + rows]
    box = box + column_shift(box, 1) + column_shift(box, -1)
    laplacian = inner(box - 9.0 * centre)
    centre = inner(centre)
    target = expand(on_side) * b[1:, 1:] + expand(on_image) * z[1:, 1:]
    totals = jnp.stack(
        [
            jnp.sum(centre * centre, axis=(0, 1)),
            jnp.sum(centre * laplacian, axis=(0, 1)),
            jnp.sum(laplacian * laplacian, axis=(0, 1)),
            jnp.sum(centre * target, axis=(0, 1)),
            jnp.sum(laplacian * target, axis=(0, 1)),
        ],
        0,
    )
    return posterior, fit_cells(totals)


def solution(mesh):
    placed = (
        P("day", ("region", "space"), None),
        P("day", ("region", "space"), None),
        P(("region", "space"), None),
        P(None, ("region", "space"), None),
        P(("region", "space"), None),
        P(("region", "space"), None),
        P(None, "day", ("region", "space"), None),
    )
    return jax.shard_map(
        shards,
        mesh=mesh,
        in_specs=placed,
        out_specs=(P("day", ("region", "space"), None), P(None, ("region", "space"), "day")),
        check_vma=False,
    )
```

```python
import jax
import jax.numpy as jnp
from jax import lax
from jax.experimental import pallas as pl
from jax.experimental.pallas import tpu as pltpu
from jax.sharding import PartitionSpec as P

RIDGE = 1.0
LANES = 128
FIELDS = 3
F32 = jnp.float32

M_PLANE, T_PLANE, Q_PLANE, H_PLANE, PLANES = 0, 9, 18, 21, 24


def send(x, space_of, day_of=lambda d: d):
    spaces, days = lax.axis_size("space"), lax.axis_size("day")
    pairs = []
    for s in range(spaces):
        for d in range(days):
            to_s, to_d = space_of(s), day_of(d)
            if 0 <= to_s < spaces:
                pairs.append((s * days + d, to_s * days + to_d))
    return lax.ppermute(x, ("space", "day"), pairs)


def position(axis):
    return lax.broadcasted_iota(jnp.int32, (8, LANES), axis)


def rolled(x, step, axis):
    return pltpu.roll(x, step % x.shape[axis], axis)


def tile(t):
    return pl.ds(t * LANES, LANES)


def dynamic_tile(start, t):
    return pl.ds(pl.multiple_of(start + t * LANES, LANES), LANES)


def doubled(x):
    return jnp.concatenate([x, x], 0)


class Shift:
    def __init__(self, step):
        self.step, self.edge, self.tiles = step, (0 if step > 0 else LANES - 1), []

    def push(self, x):
        self.tiles.append(rolled(x, self.step, 1))

    def take(self, t):
        beside = t - self.step
        here = self.tiles[t]
        other = self.tiles[beside] if 0 <= beside < len(self.tiles) else jnp.zeros_like(here)
        return jnp.where(position(1) == self.edge, other, here)


def right_sides_kernel(observed, gap, sea, precision, noise, perturbation, mine, give):
    day = lax.axis_index("day")
    tiles = mine.shape[-1] // LANES
    reach = observed.shape[-1] - mine.shape[-1]
    for out, side in ((mine, day), (give, 1 - day)):
        start = side * reach
        for t in range(tiles):
            at = dynamic_tile(start, t)
            both = lambda ref, *lead: jnp.concatenate([ref[(*lead, 0, slice(None), at)], ref[(*lead, 1, slice(None), at)]], 0)
            wet = doubled(sea[:, at].astype(F32))
            seen = doubled(noise[:, at]) * both(gap).astype(F32)
            base = wet * seen * both(observed)
            spread = wet * jnp.sqrt(doubled(precision[:, at]) + seen)
            out[0, :, tile(t)] = base
            out[1, :, tile(t)] = base + spread * both(perturbation, 0).astype(F32)
            out[2, :, tile(t)] = base + spread * both(perturbation, 1).astype(F32)
            out[3, :, tile(t)] = seen


def coefficients_kernel(stencil, sea, precision, planes, cells):
    day = lax.axis_index("day")
    width = planes.shape[-1]
    tiles = width // LANES
    start = day * (stencil.shape[-1] - width)
    row = position(0) % 4
    shifts = {(a, c): Shift(c) for a in (-1, 0, 1) for c in (-1, 1)}
    for t in range(tiles + 1):
        if t < tiles:
            at = dynamic_tile(start, t)
            cells[0, :, tile(t)] = doubled(sea[:, at].astype(F32))
            cells[1, :, tile(t)] = doubled(precision[:, at])
            own = {}
            for a in (-1, 0, 1):
                for c in (-1, 0, 1):
                    k = 3 * (a + 1) + c + 1
                    s = doubled(stencil[k, :, at].astype(F32))
                    own[a, c] = s
                    moved = s if a == 0 else jnp.where(row == (0 if a > 0 else 3), 0.0, rolled(s, a, 0))
                    planes[T_PLANE + k, :, tile(t)] = moved
                    if c == 0:
                        planes[M_PLANE + k, :, tile(t)] = s
                    else:
                        shifts[a, c].push(s)
            for c in (-1, 0, 1):
                planes[Q_PLANE + c + 1, :, tile(t)] = jnp.where(row == 0, own[-1, c], jnp.where(row == 3, own[1, c], 0.0))
            planes[H_PLANE + 1, :, tile(t)] = jnp.where(row == 0, own[-1, 0], jnp.where(row == 3, own[1, 0], 0.0))
        if t >= 1:
            for c in (-1, 1):
                got = {}
                for a in (-1, 0, 1):
                    got[a] = shifts[a, c].take(t - 1)
                    planes[M_PLANE + 3 * (a + 1) + c + 1, :, tile(t - 1)] = got[a]
                planes[H_PLANE + c + 1, :, tile(t - 1)] = jnp.where(row == 0, got[-1], jnp.where(row == 3, got[1], 0.0))


def edges_kernel(mine, got, cells, to_below, to_above):
    day = lax.axis_index("day")
    for which in (0, 1):
        early, late = ((mine, got), (got, mine))[which]

        @pl.when(day == which)
        def _():
            for out, r in ((to_below, 3), (to_above, 0)):
                for f in range(FIELDS):
                    out[3 * f, :, :] = early[f, r : r + 1, :]
                    out[3 * f + 1, :, :] = early[f, 4 + r : 5 + r, :]
                    out[3 * f + 2, :, :] = late[f, r : r + 1, :]

    to_below[9, :, :] = cells[0, 3:4, :]
    to_above[9, :, :] = cells[0, 0:1, :]


def apply_rows(planes, at, base, terms):
    sums = []
    for c in (0, 1, 2):
        total = planes[base + c, :, at] * terms[0]
        total = total + planes[base + 3 + c, :, at] * terms[1]
        total = total + planes[base + 6 + c, :, at] * terms[2]
        sums.append(total)
    return sums


def inside_kernel(mine, got, planes, pairs, moved):
    day = lax.axis_index("day")
    tiles = mine.shape[-1] // LANES
    row = position(0) % 4
    first = day == 0
    for f in range(FIELDS + 1):
        for half in (0, 1):
            shifts = (Shift(1), Shift(-1))
            middle = []
            for t in range(tiles + 1):
                if t < tiles:
                    x, y = mine[f, :, tile(t)], got[f, :, tile(t)]
                    u = jnp.where(first, x, y) if half == 0 else jnp.where(first, y, x)
                    pairs[half, f, :, tile(t)] = u
                    if f < FIELDS:
                        up = jnp.where(row == 0, 0.0, rolled(u, 1, 0))
                        down = jnp.where(row == 3, 0.0, rolled(u, -1, 0))
                        left, centre, right = apply_rows(planes, tile(t), M_PLANE, (up, u, down))
                        shifts[0].push(left)
                        shifts[1].push(right)
                        middle.append(centre)
                if t >= 1 and f < FIELDS:
                    moved[half, f, :, tile(t - 1)] = middle[t - 1] + shifts[0].take(t - 1) + shifts[1].take(t - 1)


def placed(above, below, index, at):
    row = position(0)
    spread = lambda ref, k: jnp.broadcast_to(ref[k, :, at], (8, LANES))
    first, second = index
    out = jnp.where(row < 2, spread(above, first), spread(below, first))
    if second is not None:
        late = jnp.where(row < 6, spread(above, second), spread(below, second))
        out = jnp.where(row < 4, out, late)
    return out


def split_rows(below, above, plane, x, at, first, second):
    if first is not None:
        above[plane + first, :, at] = x[0:1]
        below[plane + first, :, at] = x[3:4]
    if second is not None:
        above[plane + second, :, at] = x[4:5]
        below[plane + second, :, at] = x[7:8]


def image_kernel(pairs, moved, planes, cells, above, below, image, rims, to_below, to_above):
    tiles = moved.shape[-1] // LANES
    row = position(0)
    low = row < 4
    for f in range(FIELDS):
        incoming = [(Shift(1), Shift(-1)) for _ in (0, 1)]
        scatter = [(Shift(-1), Shift(1)) for _ in (0, 1)]
        leaving = [(Shift(-1), Shift(1)) for _ in (0, 1)]
        kept = {}
        for t in range(tiles + 2):
            if t < tiles:
                at = tile(t)
                for half in (0, 1):
                    rim = placed(above, below, (3 * f, 3 * f + 1) if half == 0 else (3 * f + 2, None), at)
                    if f > 0:
                        rims[half, f - 1, :, at] = rim
                    incoming[half][0].push(planes[H_PLANE, :, at] * rim)
                    kept["in", half, t] = planes[H_PLANE + 1, :, at] * rim
                    incoming[half][1].push(planes[H_PLANE + 2, :, at] * rim)
            if 1 <= t <= tiles:
                q = t - 1
                at = tile(q)
                m = [
                    moved[half, f, :, at] + kept.pop(("in", half, q)) + incoming[half][0].take(q) + incoming[half][1].take(q)
                    for half in (0, 1)
                ]
                before = (jnp.where(low, 0.0, rolled(m[0], 4, 0)), rolled(jnp.where(low, m[1], m[0]), 4, 0))
                for half in (0, 1):
                    u = pairs[half, f, :, at]
                    w = cells[1, :, at] * (u - before[half])
                    left, centre, right = apply_rows(planes, at, T_PLANE, (rolled(w, -1, 0), w, rolled(w, 1, 0)))
                    scatter[half][0].push(left)
                    scatter[half][1].push(right)
                    leaving[half][0].push(planes[Q_PLANE, :, at] * w)
                    leaving[half][1].push(planes[Q_PLANE + 2, :, at] * w)
                    kept[half, q] = (w + pairs[half, FIELDS, :, at] * u, centre, planes[Q_PLANE + 1, :, at] * w)
            if t >= 2:
                q = t - 2
                at = tile(q)
                s, out = [], []
                for half in (0, 1):
                    own, centre, edge = kept.pop((half, q))
                    s.append(centre + scatter[half][0].take(q) + scatter[half][1].take(q))
                    out.append(edge + leaving[half][0].take(q) + leaving[half][1].take(q))
                    kept["own", half] = own
                after = (rolled(jnp.where(low, s[1], s[0]), 4, 0), jnp.where(low, rolled(s[1], 4, 0), 0.0))
                for half in (0, 1):
                    z = cells[0, :, at] * (kept.pop(("own", half)) - after[half])
                    image[half, f, :, at] = z
                    split_rows(to_below, to_above, 0, z, at, 3 * f + 2 * half, 3 * f + 1 if half == 0 else None)
                split_rows(to_below, to_above, 9, out[0], at, None, 3 * f)
                split_rows(to_below, to_above, 9, out[1], at, 3 * f + 1, 3 * f + 2)


def sums_kernel(pairs, part, planes, cells, sea_above, sea_below, to_below, to_above, above, below, image, rims, swap):
    day = lax.axis_index("day")
    tiles = part.shape[-1] // LANES
    row = position(0)
    low = row < 4
    edge = (row % 4 == 0) | (row % 4 == 3)
    rows = []
    for f in range(FIELDS):
        shifts = [(Shift(1), Shift(-1)) for _ in (0, 1)]
        kept = {}
        totals = [None] * 4
        for t in range(tiles + 1):
            if t < tiles:
                at = tile(t)
                wet = cells[0, :, at]
                wet_rim = placed(sea_above, sea_below, (9, 9), at)
                for half in (0, 1):
                    days = (3 * f, 3 * f + 1) if half == 0 else (3 * f + 2, None)
                    late = tuple(None if k is None else 9 + k for k in days)
                    came = placed(above, below, late, at)
                    keep = edge if half == 0 else edge & low
                    z = part[half, f, :, at] - jnp.where(keep, wet * came, 0.0)
                    rim = placed(above, below, days, at) - wet_rim * placed(to_above, to_below, late, at)
                    image[half, f, :, at] = z
                    if f > 0:
                        rims[half, f - 1, :, at] = rim
                    up = jnp.where(row % 4 == 0, rim, rolled(z, 1, 0))
                    down = jnp.where(row % 4 == 3, rim, rolled(z, -1, 0))
                    left, centre, right = apply_rows(planes, at, M_PLANE, (up, z, down))
                    shifts[half][0].push(left)
                    shifts[half][1].push(right)
                    kept[half, t] = (z, centre)
            if t >= 1:
                q = t - 1
                at = tile(q)
                z, m = [], []
                for half in (0, 1):
                    own, centre = kept.pop((half, q))
                    z.append(own)
                    m.append(centre + shifts[half][0].take(q) + shifts[half][1].take(q))
                before = (jnp.where(low, 0.0, rolled(m[0], 4, 0)), rolled(jnp.where(low, m[1], m[0]), 4, 0))
                terms = [0.0] * 4
                for half in (0, 1):
                    b = pairs[half, f, :, at]
                    gap = z[half] - before[half]
                    terms[0] = terms[0] + b * b
                    terms[1] = terms[1] + b * z[half]
                    terms[2] = terms[2] + z[half] * z[half]
                    terms[3] = terms[3] + (cells[1, :, at] * gap * gap + pairs[half, FIELDS, :, at] * z[half] * z[half])
                if q == 0:
                    terms = [jnp.where(day == 0, x, 0.0) for x in terms]
                elif q == tiles - 1:
                    terms = [jnp.where(day == 0, 0.0, x) for x in terms]
                totals = [x if y is None else x + y for x, y in zip(terms, totals)]
        rows += [jnp.sum(x, axis=0, keepdims=True) for x in totals]
    for k, x in enumerate(rows):
        swap[tiles - 1 + k // 8, k % 8 : k % 8 + 1, :] = x
    swap[tiles, 4:8, :] = jnp.zeros((4, LANES), F32)
    for which in (0, 1):

        @pl.when(day == which)
        def _():
            for t in range(tiles - 1):
                swap[t, :, :] = image[1 - which, 0, :, tile(t + which)]


def fit_kernel(scalars, mine, give, pairs, image, theirs, side_rims, image_rims, posterior, fitted):
    day = lax.axis_index("day")
    tiles = mine.shape[-1] // LANES
    row = position(0)
    low = row < 4
    weights = []
    for f in range(FIELDS):
        m = []
        for k in range(4 * f, 4 * f + 4):
            total = jnp.sum(scalars[k // 8, k % 8 : k % 8 + 1, :], axis=1, keepdims=True)
            m.append(jnp.broadcast_to(total, (8, LANES)))
        step = m[0] / m[1]
        norm_next = step * step * m[2] - m[0]
        grown = 1.0 + norm_next / m[0]
        curvature = grown * grown * m[1] - 2.0 * step * grown * m[2] + step * step * m[3]
        second = norm_next / curvature
        weights.append((step + second * grown, -second * step))

    def store(at, x):
        posterior[0, :, at] = x[0:4]
        posterior[1, :, at] = x[4:8]

    on_side, on_image = weights[0]
    for which in (0, 1):

        @pl.when(day == which)
        def _():
            for t in range(tiles - 1):
                here, there = which * (tiles - 1), (1 - which) * (tiles - 1)
                own = on_side * mine[0, :, tile(t + which)] + on_image * image[which, 0, :, tile(t + which)]
                store(tile(here + t), own)
                store(tile(there + t), on_side * give[0, :, tile(t + 1 - which)] + on_image * theirs[t, :, :])

    wide = {(f, half): (Shift(1), Shift(-1)) for f in (1, 2) for half in (0, 1)}
    kept = {}
    for t in range(tiles + 1):
        if t < tiles:
            at = tile(t)
            for f in (1, 2):
                on_side, on_image = weights[f]
                for half in (0, 1):
                    x = on_side * pairs[half, f, :, at] + on_image * image[half, f, :, at]
                    rim = on_side * side_rims[half, f - 1, :, at] + on_image * image_rims[half, f - 1, :, at]
                    up = jnp.where(row % 4 == 0, rim, rolled(x, 1, 0))
                    down = jnp.where(row % 4 == 3, rim, rolled(x, -1, 0))
                    box = x + up + down
                    wide[f, half][0].push(box)
                    wide[f, half][1].push(box)
                    kept[f, half, t] = (x, box)
        if t >= 1:
            q = t - 1
            totals = [0.0] * 5
            for f in (1, 2):
                (x0, box0), (x1, box1) = kept.pop((f, 0, q)), kept.pop((f, 1, q))
                targets = (rolled(jnp.where(low, x1, x0), 4, 0), rolled(x1, 4, 0))
                for half, (x, box) in enumerate(((x0, box0), (x1, box1))):
                    lap = box + wide[f, half][0].take(q) + wide[f, half][1].take(q) - 9.0 * x
                    if half == 1:
                        x, lap = jnp.where(low, x, 0.0), jnp.where(low, lap, 0.0)
                    target = targets[half]
                    for k, term in enumerate((x * x, x * lap, lap * lap, x * target, lap * target)):
                        totals[k] = totals[k] + term
            m = [x + rolled(x, 4, 0) for x in totals]
            first, second = m[0] + RIDGE, m[2] + RIDGE
            inverse = 1.0 / (first * second - m[1] * m[1])
            persistence = (second * m[3] - m[1] * m[4]) * inverse
            diffusion = (first * m[4] - m[1] * m[3]) * inverse

            def write(to):
                fitted[0, :, tile(to)] = persistence[0:4]
                fitted[1, :, tile(to)] = diffusion[0:4]

            if q < tiles - 1:
                pl.when(day == 0)(lambda: write(q))
            if q > 0:
                pl.when(day == 1)(lambda: write(q - 1))


def call(kernel, outs, *args, flops=2_000_000):
    vmem = pl.BlockSpec(memory_space=pltpu.VMEM)
    size = sum(x.size * x.dtype.itemsize for x in args)
    return pl.pallas_call(
        kernel,
        out_shape=[jax.ShapeDtypeStruct(s, F32) for s in outs],
        in_specs=[vmem] * len(args),
        out_specs=[vmem] * len(outs),
        cost_estimate=pl.CostEstimate(flops=flops, bytes_accessed=size, transcendentals=0),
        compiler_params=pltpu.CompilerParams(vmem_limit_bytes=32 << 20),
    )(*args)


def shards(observed, gap_mask, sea_mask, stencil, precision, noise_precision, perturbation):
    cols = observed.shape[-1]
    spaces = lax.axis_size("space")
    half = cols // 2
    width = half + LANES
    tiles = width // LANES
    pair = (8, width)

    mine, give = call(
        right_sides_kernel, [(4, *pair)] * 2, observed, gap_mask, sea_mask, precision, noise_precision, perturbation
    )
    got = send(give, lambda s: s, lambda d: 1 - d)
    planes, cells = call(coefficients_kernel, [(PLANES, *pair), (2, *pair)], stencil, sea_mask, precision)
    to_below, to_above = call(edges_kernel, [(10, 1, width)] * 2, mine, got, cells)
    above = send(to_below, lambda s: s + 1)
    below = send(to_above, lambda s: s - 1)
    pairs, moved = call(inside_kernel, [(2, 4, *pair), (2, 3, *pair)], mine, got, planes)
    part, side_rims, to_below, to_above = call(
        image_kernel, [(2, 3, *pair), (2, 2, *pair), (18, 1, width), (18, 1, width)], pairs, moved, planes, cells, above, below
    )
    from_above = send(to_below, lambda s: s + 1)
    from_below = send(to_above, lambda s: s - 1)
    image, image_rims, swap = call(
        sums_kernel,
        [(2, 3, *pair), (2, 2, *pair), (tiles + 1, 8, LANES)],
        pairs, part, planes, cells, above, below, to_below, to_above, from_above, from_below,
    )
    theirs = send(swap, lambda s: s, lambda d: 1 - d)
    scalars = swap[tiles - 1 :]
    if spaces & (spaces - 1) == 0:
        scalars = scalars + theirs[tiles - 1 :]
        bit = 1
        while bit < spaces:
            scalars = scalars + send(scalars, lambda s: s ^ bit)
            bit *= 2
    else:
        scalars = lax.psum(scalars, ("space", "day"))
    posterior, fitted = call(
        fit_kernel,
        [observed.shape, (2, observed.shape[1], half)],
        scalars, mine, give, pairs, image, theirs, side_rims, image_rims,
    )
    return posterior, fitted


def solution(mesh):
    placed_args = (
        P("day", ("region", "space"), None),
        P("day", ("region", "space"), None),
        P(("region", "space"), None),
        P(None, ("region", "space"), None),
        P(("region", "space"), None),
        P(("region", "space"), None),
        P(None, "day", ("region", "space"), None),
    )
    return jax.shard_map(
        shards,
        mesh=mesh,
        in_specs=placed_args,
        out_specs=(P("day", ("region", "space"), None), P(None, ("region", "space"), "day")),
        check_vma=False,
    )
```

```python
import jax
import jax.numpy as jnp
from jax import lax
from jax.experimental import pallas as pl
from jax.experimental.pallas import tpu as pltpu
from jax.sharding import PartitionSpec as P

RIDGE = 1.0
LANES = 128
FIELDS = 3
F32 = jnp.float32

M_PLANE, T_PLANE, Q_PLANE, H_PLANE, PLANES = 0, 9, 18, 21, 24


def send(x, space_of, day_of=lambda d: d):
    spaces, days = lax.axis_size("space"), lax.axis_size("day")
    pairs = []
    for s in range(spaces):
        for d in range(days):
            to_s, to_d = space_of(s), day_of(d)
            if 0 <= to_s < spaces:
                pairs.append((s * days + d, to_s * days + to_d))
    return lax.ppermute(x, ("space", "day"), pairs)


def position(axis):
    return lax.broadcasted_iota(jnp.int32, (8, LANES), axis)


def rolled(x, step, axis):
    return pltpu.roll(x, step % x.shape[axis], axis)


def tile(t):
    return pl.ds(t * LANES, LANES)


def dynamic_tile(start, t):
    return pl.ds(pl.multiple_of(start + t * LANES, LANES), LANES)


def doubled(x):
    return jnp.concatenate([x, x], 0)


class Shift:
    def __init__(self, step):
        self.step, self.edge, self.tiles = step, (0 if step > 0 else LANES - 1), []

    def push(self, x):
        self.tiles.append(rolled(x, self.step, 1))

    def take(self, t):
        beside = t - self.step
        here = self.tiles[t]
        other = self.tiles[beside] if 0 <= beside < len(self.tiles) else jnp.zeros_like(here)
        return jnp.where(position(1) == self.edge, other, here)


def fetch(sources, buffers, semaphores):
    copies = [pltpu.make_async_copy(x, y, semaphores.at[k]) for k, (x, y) in enumerate(zip(sources, buffers))]
    for copy in copies:
        copy.start()
    for copy in copies:
        copy.wait()


def right_sides_kernel(*refs):
    sources, (mine, give), buffers, semaphores = refs[:6], refs[6:8], refs[8:14], refs[14]
    fetch(sources, buffers, semaphores)
    observed, gap, sea, precision, noise, perturbation = buffers
    day = lax.axis_index("day")
    tiles = mine.shape[-1] // LANES
    reach = observed.shape[-1] - mine.shape[-1]
    for out, side in ((mine, day), (give, 1 - day)):
        start = side * reach
        for t in range(tiles):
            at = dynamic_tile(start, t)
            both = lambda ref, *lead: jnp.concatenate([ref[(*lead, 0, slice(None), at)], ref[(*lead, 1, slice(None), at)]], 0)
            wet = doubled(sea[:, at].astype(F32))
            seen = doubled(noise[:, at]) * both(gap).astype(F32)
            base = wet * seen * both(observed)
            spread = wet * jnp.sqrt(doubled(precision[:, at]) + seen)
            out[0, :, tile(t)] = base
            out[1, :, tile(t)] = base + spread * both(perturbation, 0).astype(F32)
            out[2, :, tile(t)] = base + spread * both(perturbation, 1).astype(F32)
            out[3, :, tile(t)] = seen


def coefficients_kernel(*refs):
    sources, (planes, cells), buffers, semaphores = refs[:3], refs[3:5], refs[5:8], refs[8]
    fetch(sources, buffers, semaphores)
    stencil, sea, precision = buffers
    day = lax.axis_index("day")
    width = planes.shape[-1]
    tiles = width // LANES
    start = day * (stencil.shape[-1] - width)
    row = position(0) % 4
    shifts = {(a, c): Shift(c) for a in (-1, 0, 1) for c in (-1, 1)}
    for t in range(tiles + 1):
        if t < tiles:
            at = dynamic_tile(start, t)
            cells[0, :, tile(t)] = doubled(sea[:, at].astype(F32))
            cells[1, :, tile(t)] = doubled(precision[:, at])
            own = {}
            for a in (-1, 0, 1):
                for c in (-1, 0, 1):
                    k = 3 * (a + 1) + c + 1
                    s = doubled(stencil[k, :, at].astype(F32))
                    own[a, c] = s
                    moved = s if a == 0 else jnp.where(row == (0 if a > 0 else 3), 0.0, rolled(s, a, 0))
                    planes[T_PLANE + k, :, tile(t)] = moved
                    if c == 0:
                        planes[M_PLANE + k, :, tile(t)] = s
                    else:
                        shifts[a, c].push(s)
            for c in (-1, 0, 1):
                planes[Q_PLANE + c + 1, :, tile(t)] = jnp.where(row == 0, own[-1, c], jnp.where(row == 3, own[1, c], 0.0))
            planes[H_PLANE + 1, :, tile(t)] = jnp.where(row == 0, own[-1, 0], jnp.where(row == 3, own[1, 0], 0.0))
        if t >= 1:
            for c in (-1, 1):
                got = {}
                for a in (-1, 0, 1):
                    got[a] = shifts[a, c].take(t - 1)
                    planes[M_PLANE + 3 * (a + 1) + c + 1, :, tile(t - 1)] = got[a]
                planes[H_PLANE + c + 1, :, tile(t - 1)] = jnp.where(row == 0, got[-1], jnp.where(row == 3, got[1], 0.0))


def even_strip():
    return lax.axis_index("space") % 2 == 0


def pack_rows(plane, blocks, paired, crossed):
    for even in (True, False):
        to_below, to_above = (paired, crossed) if even else (crossed, paired)

        @pl.when(even_strip() == even)
        def _():
            for out, r in ((to_below, 3), (to_above, 0)):
                for f in range(FIELDS):
                    early, late = blocks(f)
                    out[plane + 3 * f, :, :] = early[r : r + 1, :]
                    out[plane + 3 * f + 1, :, :] = early[4 + r : 5 + r, :]
                    out[plane + 3 * f + 2, :, :] = late[r : r + 1, :]


def unpack_rows(paired, crossed, above, below):
    for even in (True, False):

        @pl.when(even_strip() == even)
        def _():
            below[...] = (paired if even else crossed)[...]
            above[...] = (crossed if even else paired)[...]


def edges_kernel(mine, got, cells, paired, crossed):
    for day in (0, 1):

        @pl.when(lax.axis_index("day") == day)
        def _():
            early, late = (mine, got) if day == 0 else (got, mine)
            pack_rows(0, lambda f: (early.at[f], late.at[f]), paired, crossed)

    for even in (True, False):

        @pl.when(even_strip() == even)
        def _():
            paired[9, :, :] = cells[0, 3:4, :] if even else cells[0, 0:1, :]
            crossed[9, :, :] = cells[0, 0:1, :] if even else cells[0, 3:4, :]


def apply_rows(planes, at, base, terms):
    sums = []
    for c in (0, 1, 2):
        total = planes[base + c, :, at] * terms[0]
        total = total + planes[base + 3 + c, :, at] * terms[1]
        total = total + planes[base + 6 + c, :, at] * terms[2]
        sums.append(total)
    return sums


def inside_kernel(mine, got, planes, pairs, moved):
    day = lax.axis_index("day")
    tiles = mine.shape[-1] // LANES
    row = position(0) % 4
    first = day == 0
    for f in range(FIELDS + 1):
        for half in (0, 1):
            shifts = (Shift(1), Shift(-1))
            middle = []
            for t in range(tiles + 1):
                if t < tiles:
                    x, y = mine[f, :, tile(t)], got[f, :, tile(t)]
                    u = jnp.where(first, x, y) if half == 0 else jnp.where(first, y, x)
                    pairs[half, f, :, tile(t)] = u
                    if f < FIELDS:
                        up = jnp.where(row == 0, 0.0, rolled(u, 1, 0))
                        down = jnp.where(row == 3, 0.0, rolled(u, -1, 0))
                        left, centre, right = apply_rows(planes, tile(t), M_PLANE, (up, u, down))
                        shifts[0].push(left)
                        shifts[1].push(right)
                        middle.append(centre)
                if t >= 1 and f < FIELDS:
                    moved[half, f, :, tile(t - 1)] = middle[t - 1] + shifts[0].take(t - 1) + shifts[1].take(t - 1)


def placed(above, below, index, at):
    row = position(0)
    spread = lambda ref, k: jnp.broadcast_to(ref[k, :, at], (8, LANES))
    first, second = index
    out = jnp.where(row < 2, spread(above, first), spread(below, first))
    if second is not None:
        late = jnp.where(row < 6, spread(above, second), spread(below, second))
        out = jnp.where(row < 4, out, late)
    return out


def image_kernel(pairs, moved, planes, cells, came_paired, came_crossed, image, leaves, rims, paired, crossed, above, below):
    unpack_rows(came_paired, came_crossed, above, below)
    tiles = moved.shape[-1] // LANES
    row = position(0)
    low = row < 4
    for f in range(FIELDS):
        incoming = [(Shift(1), Shift(-1)) for _ in (0, 1)]
        scatter = [(Shift(-1), Shift(1)) for _ in (0, 1)]
        leaving = [(Shift(-1), Shift(1)) for _ in (0, 1)]
        kept = {}
        for t in range(tiles + 2):
            if t < tiles:
                at = tile(t)
                for half in (0, 1):
                    rim = placed(above, below, (3 * f, 3 * f + 1) if half == 0 else (3 * f + 2, None), at)
                    if f > 0:
                        rims[half, f - 1, :, at] = rim
                    incoming[half][0].push(planes[H_PLANE, :, at] * rim)
                    kept["in", half, t] = planes[H_PLANE + 1, :, at] * rim
                    incoming[half][1].push(planes[H_PLANE + 2, :, at] * rim)
            if 1 <= t <= tiles:
                q = t - 1
                at = tile(q)
                m = [
                    moved[half, f, :, at] + kept.pop(("in", half, q)) + incoming[half][0].take(q) + incoming[half][1].take(q)
                    for half in (0, 1)
                ]
                before = (jnp.where(low, 0.0, rolled(m[0], 4, 0)), rolled(jnp.where(low, m[1], m[0]), 4, 0))
                for half in (0, 1):
                    u = pairs[half, f, :, at]
                    w = cells[1, :, at] * (u - before[half])
                    left, centre, right = apply_rows(planes, at, T_PLANE, (rolled(w, -1, 0), w, rolled(w, 1, 0)))
                    scatter[half][0].push(left)
                    scatter[half][1].push(right)
                    leaving[half][0].push(planes[Q_PLANE, :, at] * w)
                    leaving[half][1].push(planes[Q_PLANE + 2, :, at] * w)
                    kept[half, q] = (w + pairs[half, FIELDS, :, at] * u, centre, planes[Q_PLANE + 1, :, at] * w)
            if t >= 2:
                q = t - 2
                at = tile(q)
                s, out = [], []
                for half in (0, 1):
                    own, centre, edge = kept.pop((half, q))
                    s.append(centre + scatter[half][0].take(q) + scatter[half][1].take(q))
                    out.append(edge + leaving[half][0].take(q) + leaving[half][1].take(q))
                    kept["own", half] = own
                after = (rolled(jnp.where(low, s[1], s[0]), 4, 0), jnp.where(low, rolled(s[1], 4, 0), 0.0))
                leaves[0, f, :, at] = rolled(jnp.where(low, out[1], out[0]), 4, 0)
                leaves[1, f, :, at] = rolled(out[1], 4, 0)
                for half in (0, 1):
                    image[half, f, :, at] = cells[0, :, at] * (kept.pop(("own", half)) - after[half])
    pack_rows(0, lambda f: (image.at[0, f], image.at[1, f]), paired, crossed)
    pack_rows(9, lambda f: (leaves.at[0, f], leaves.at[1, f]), paired, crossed)


def sums_kernel(*refs):
    pairs, part, leaves, planes, cells, first_paired, first_crossed, came_paired, came_crossed = refs[:9]
    image, rims, swap, sums, sea_above, sea_below, above, below = refs[9:]
    unpack_rows(first_paired.at[9:10], first_crossed.at[9:10], sea_above, sea_below)
    unpack_rows(came_paired, came_crossed, above, below)
    day = lax.axis_index("day")
    tiles = part.shape[-1] // LANES
    row = position(0)
    low = row < 4
    edge = (row % 4 == 0) | (row % 4 == 3)
    rows = []
    for f in range(FIELDS):
        shifts = [(Shift(1), Shift(-1)) for _ in (0, 1)]
        kept = {}
        totals = [None] * 4
        for t in range(tiles + 1):
            if t < tiles:
                at = tile(t)
                wet = cells[0, :, at]
                wet_rim = placed(sea_above, sea_below, (0, 0), at)
                for half in (0, 1):
                    days = (3 * f, 3 * f + 1) if half == 0 else (3 * f + 2, None)
                    late = tuple(None if k is None else 9 + k for k in days)
                    came = placed(above, below, late, at)
                    keep = edge if half == 0 else edge & low
                    z = part[half, f, :, at] - jnp.where(keep, wet * came, 0.0)
                    rim = placed(above, below, days, at) - wet_rim * leaves[half, f, :, at]
                    image[half, f, :, at] = z
                    if f > 0:
                        rims[half, f - 1, :, at] = rim
                    up = jnp.where(row % 4 == 0, rim, rolled(z, 1, 0))
                    down = jnp.where(row % 4 == 3, rim, rolled(z, -1, 0))
                    left, centre, right = apply_rows(planes, at, M_PLANE, (up, z, down))
                    shifts[half][0].push(left)
                    shifts[half][1].push(right)
                    kept[half, t] = (z, centre)
            if t >= 1:
                q = t - 1
                at = tile(q)
                z, m = [], []
                for half in (0, 1):
                    own, centre = kept.pop((half, q))
                    z.append(own)
                    m.append(centre + shifts[half][0].take(q) + shifts[half][1].take(q))
                before = (jnp.where(low, 0.0, rolled(m[0], 4, 0)), rolled(jnp.where(low, m[1], m[0]), 4, 0))
                terms = [0.0] * 4
                for half in (0, 1):
                    b = pairs[half, f, :, at]
                    gap = z[half] - before[half]
                    terms[0] = terms[0] + b * b
                    terms[1] = terms[1] + b * z[half]
                    terms[2] = terms[2] + z[half] * z[half]
                    terms[3] = terms[3] + (cells[1, :, at] * gap * gap + pairs[half, FIELDS, :, at] * z[half] * z[half])
                if q == 0:
                    terms = [jnp.where(day == 0, x, 0.0) for x in terms]
                elif q == tiles - 1:
                    terms = [jnp.where(day == 0, 0.0, x) for x in terms]
                totals = [x if y is None else x + y for x, y in zip(terms, totals)]
        rows += [jnp.sum(jnp.sum(x, axis=0, keepdims=True), axis=1, keepdims=True) for x in totals]
    lane = lax.broadcasted_iota(jnp.int32, (1, LANES), 1)
    line = jnp.zeros((1, LANES), F32)
    for k, x in enumerate(rows):
        line = jnp.where(lane == k, x, line)
    for k in range(sums.shape[0]):
        sums[k, :, :] = line
    for which in (0, 1):

        @pl.when(day == which)
        def _():
            for t in range(tiles - 1):
                swap[t, :, :] = image[1 - which, 0, :, tile(t + which)]


def fit_kernel(sums, mine, give, pairs, image, theirs, side_rims, image_rims, posterior, fitted, mean, cells, ready, semaphores):
    day = lax.axis_index("day")
    tiles = mine.shape[-1] // LANES
    row = position(0)
    low = row < 4
    line = sums[0, :, :]
    for k in range(1, sums.shape[0]):
        line = line + sums[k, :, :]
    weights = []
    for f in range(FIELDS):
        m = [jnp.broadcast_to(line[:, k : k + 1], (8, LANES)) for k in range(4 * f, 4 * f + 4)]
        step = m[0] / m[1]
        norm_next = step * step * m[2] - m[0]
        grown = 1.0 + norm_next / m[0]
        curvature = grown * grown * m[1] - 2.0 * step * grown * m[2] + step * step * m[3]
        second = norm_next / curvature
        weights.append((step + second * grown, -second * step))

    def store(at, x):
        mean[0, :, at] = x[0:4]
        mean[1, :, at] = x[4:8]

    on_side, on_image = weights[0]
    for which in (0, 1):

        @pl.when(day == which)
        def _():
            for t in range(tiles - 1):
                here, there = which * (tiles - 1), (1 - which) * (tiles - 1)
                own = on_side * mine[0, :, tile(t + which)] + on_image * image[which, 0, :, tile(t + which)]
                store(tile(here + t), own)
                store(tile(there + t), on_side * give[0, :, tile(t + 1 - which)] + on_image * theirs[t, :, :])

    out_mean = pltpu.make_async_copy(mean, posterior, semaphores.at[0])
    out_mean.start()

    wide = {(f, half): (Shift(1), Shift(-1)) for f in (1, 2) for half in (0, 1)}
    kept = {}
    for t in range(tiles + 1):
        if t < tiles:
            at = tile(t)
            for f in (1, 2):
                on_side, on_image = weights[f]
                for half in (0, 1):
                    x = on_side * pairs[half, f, :, at] + on_image * image[half, f, :, at]
                    rim = on_side * side_rims[half, f - 1, :, at] + on_image * image_rims[half, f - 1, :, at]
                    up = jnp.where(row % 4 == 0, rim, rolled(x, 1, 0))
                    down = jnp.where(row % 4 == 3, rim, rolled(x, -1, 0))
                    box = x + up + down
                    wide[f, half][0].push(box)
                    wide[f, half][1].push(box)
                    kept[f, half, t] = (x, box)
        if t >= 1:
            q = t - 1
            totals = [0.0] * 5
            for f in (1, 2):
                (x0, box0), (x1, box1) = kept.pop((f, 0, q)), kept.pop((f, 1, q))
                targets = (rolled(jnp.where(low, x1, x0), 4, 0), rolled(x1, 4, 0))
                for half, (x, box) in enumerate(((x0, box0), (x1, box1))):
                    lap = box + wide[f, half][0].take(q) + wide[f, half][1].take(q) - 9.0 * x
                    if half == 1:
                        x, lap = jnp.where(low, x, 0.0), jnp.where(low, lap, 0.0)
                    target = targets[half]
                    for k, term in enumerate((x * x, x * lap, lap * lap, x * target, lap * target)):
                        totals[k] = totals[k] + term
            m = [x + rolled(x, 4, 0) for x in totals]
            first, second = m[0] + RIDGE, m[2] + RIDGE
            inverse = 1.0 / (first * second - m[1] * m[1])
            persistence = (second * m[3] - m[1] * m[4]) * inverse
            diffusion = (first * m[4] - m[1] * m[3]) * inverse

            cells[0, :, tile(q)] = persistence[0:4]
            cells[1, :, tile(q)] = diffusion[0:4]
    for which in (0, 1):

        @pl.when(day == which)
        def _():
            ready[...] = cells[:, :, which * LANES : which * LANES + ready.shape[-1]]

    out_fit = pltpu.make_async_copy(ready, fitted, semaphores.at[1])
    out_fit.start()
    out_mean.wait()
    out_fit.wait()


VMEM = pl.BlockSpec(memory_space=pltpu.VMEM)
HBM = pl.BlockSpec(memory_space=pltpu.HBM)


def call(kernel, outs, *args, scratch=(), source=VMEM, target=VMEM, flops=2_000_000):
    size = sum(x.size * x.dtype.itemsize for x in args)
    return pl.pallas_call(
        kernel,
        out_shape=[jax.ShapeDtypeStruct(shape, F32) for shape in outs],
        in_specs=[source] * len(args),
        out_specs=[target] * len(outs),
        scratch_shapes=scratch,
        cost_estimate=pl.CostEstimate(flops=flops, bytes_accessed=size, transcendentals=0),
        compiler_params=pltpu.CompilerParams(vmem_limit_bytes=32 << 20),
    )(*args)


def buffers(*args):
    return [pltpu.VMEM(x.shape, x.dtype) for x in args] + [pltpu.SemaphoreType.DMA((len(args),))]


def shards(observed, gap_mask, sea_mask, stencil, precision, noise_precision, perturbation):
    cols = observed.shape[-1]
    devices = lax.axis_size("space") * lax.axis_size("day")
    half = cols // 2
    width = half + LANES
    pair = (8, width)
    row = (1, width)
    same = lambda s: s
    paired_space = lambda s: s ^ 1
    crossed_space = lambda s: ((s + 1) ^ 1) - 1

    raw = (observed, gap_mask, sea_mask, precision, noise_precision, perturbation)
    mine, give = call(right_sides_kernel, [(4, *pair)] * 2, *raw, scratch=buffers(*raw), source=HBM)
    got = send(give, same, lambda d: 1 - d)
    raw = (stencil, sea_mask, precision)
    planes, cells = call(coefficients_kernel, [(PLANES, *pair), (2, *pair)], *raw, scratch=buffers(*raw), source=HBM)
    paired, crossed = call(edges_kernel, [(10, *row)] * 2, mine, got, cells)
    first_crossed = send(crossed, crossed_space)
    first_paired = send(paired, paired_space)
    pairs, moved = call(inside_kernel, [(2, 4, *pair), (2, 3, *pair)], mine, got, planes)
    part, leaves, side_rims, paired, crossed = call(
        image_kernel,
        [(2, 3, *pair), (2, 3, *pair), (2, 2, *pair), (18, *row), (18, *row)],
        pairs, moved, planes, cells, first_paired, first_crossed,
        scratch=[pltpu.VMEM((10, *row), F32)] * 2,
    )
    crossed = send(crossed, crossed_space)
    paired = send(paired, paired_space)
    image, image_rims, swap, sums = call(
        sums_kernel,
        [(2, 3, *pair), (2, 2, *pair), (half // LANES, 8, LANES), (devices, 1, LANES)],
        pairs, part, leaves, planes, cells, first_paired, first_crossed, paired, crossed,
        scratch=[pltpu.VMEM((1, *row), F32)] * 2 + [pltpu.VMEM((18, *row), F32)] * 2,
    )
    theirs = send(swap, same, lambda d: 1 - d)
    sums = lax.all_to_all(sums, ("space", "day"), 0, 0)
    fit = (2, observed.shape[1])
    posterior, fitted = call(
        fit_kernel,
        [observed.shape, (*fit, half)],
        sums, mine, give, pairs, image, theirs, side_rims, image_rims,
        scratch=[
            pltpu.VMEM(observed.shape, F32),
            pltpu.VMEM((*fit, width), F32),
            pltpu.VMEM((*fit, half), F32),
            pltpu.SemaphoreType.DMA((2,)),
        ],
        target=HBM,
    )
    return posterior, fitted


def solution(mesh):
    placed_args = (
        P("day", ("region", "space"), None),
        P("day", ("region", "space"), None),
        P(("region", "space"), None),
        P(None, ("region", "space"), None),
        P(("region", "space"), None),
        P(("region", "space"), None),
        P(None, "day", ("region", "space"), None),
    )
    return jax.shard_map(
        shards,
        mesh=mesh,
        in_specs=placed_args,
        out_specs=(P("day", ("region", "space"), None), P(None, ("region", "space"), "day")),
        check_vma=False,
    )
```

```python
import jax
import jax.numpy as jnp
from jax import lax
from jax.experimental import pallas as pl
from jax.experimental.pallas import tpu as pltpu
from jax.sharding import PartitionSpec as P

RIDGE = 1.0
LANES = 128
FIELDS = 3
F32 = jnp.float32

M_PLANE, T_PLANE, Q_PLANE, H_PLANE, PLANES = 0, 9, 18, 21, 24


def send(x, space_of, day_of=lambda d: d):
    spaces, days = lax.axis_size("space"), lax.axis_size("day")
    pairs = []
    for s in range(spaces):
        for d in range(days):
            to_s, to_d = space_of(s), day_of(d)
            if 0 <= to_s < spaces:
                pairs.append((s * days + d, to_s * days + to_d))
    return lax.ppermute(x, ("space", "day"), pairs)


def position(axis):
    return lax.broadcasted_iota(jnp.int32, (8, LANES), axis)


def rolled(x, step, axis):
    return pltpu.roll(x, step % x.shape[axis], axis)


def tile(t):
    return pl.ds(t * LANES, LANES)


def dynamic_tile(start, t):
    return pl.ds(pl.multiple_of(start + t * LANES, LANES), LANES)


def doubled(x):
    return jnp.concatenate([x, x], 0)


class Shift:
    def __init__(self, step):
        self.step, self.edge, self.tiles = step, (0 if step > 0 else LANES - 1), []

    def push(self, x):
        self.tiles.append(rolled(x, self.step, 1))

    def take(self, t):
        beside = t - self.step
        here = self.tiles[t]
        other = self.tiles[beside] if 0 <= beside < len(self.tiles) else jnp.zeros_like(here)
        return jnp.where(position(1) == self.edge, other, here)


def fetch(sources, buffers, semaphores):
    copies = [pltpu.make_async_copy(x, y, semaphores.at[k]) for k, (x, y) in enumerate(zip(sources, buffers))]
    for copy in copies:
        copy.start()
    for copy in copies:
        copy.wait()


def right_sides_kernel(*refs):
    sources, (mine, give, cells), buffers, semaphores = refs[:6], refs[6:9], refs[9:15], refs[15]
    fetch(sources, buffers, semaphores)
    observed, gap, sea, precision, noise, perturbation = buffers
    day = lax.axis_index("day")
    tiles = mine.shape[-1] // LANES
    reach = observed.shape[-1] - mine.shape[-1]
    for out, side in ((mine, day), (give, 1 - day)):
        start = side * reach
        for t in range(tiles):
            at = dynamic_tile(start, t)
            both = lambda ref, *lead: jnp.concatenate([ref[(*lead, 0, slice(None), at)], ref[(*lead, 1, slice(None), at)]], 0)
            wet = doubled(sea[:, at].astype(F32))
            if out is mine:
                cells[0, :, tile(t)] = wet
                cells[1, :, tile(t)] = doubled(precision[:, at])
            seen = doubled(noise[:, at]) * both(gap).astype(F32)
            base = wet * seen * both(observed)
            spread = wet * jnp.sqrt(doubled(precision[:, at]) + seen)
            out[0, :, tile(t)] = base
            out[1, :, tile(t)] = base + spread * both(perturbation, 0).astype(F32)
            out[2, :, tile(t)] = base + spread * both(perturbation, 1).astype(F32)
            out[3, :, tile(t)] = seen


def coefficients(stencil, planes):
    day = lax.axis_index("day")
    width = planes.shape[-1]
    tiles = width // LANES
    start = day * (stencil.shape[-1] - width)
    row = position(0) % 4
    shifts = {(a, c): Shift(c) for a in (-1, 0, 1) for c in (-1, 1)}
    for t in range(tiles + 1):
        if t < tiles:
            at = dynamic_tile(start, t)
            own = {}
            for a in (-1, 0, 1):
                for c in (-1, 0, 1):
                    k = 3 * (a + 1) + c + 1
                    s = doubled(stencil[k, :, at].astype(F32))
                    own[a, c] = s
                    moved = s if a == 0 else jnp.where(row == (0 if a > 0 else 3), 0.0, rolled(s, a, 0))
                    planes[T_PLANE + k, :, tile(t)] = moved
                    if c == 0:
                        planes[M_PLANE + k, :, tile(t)] = s
                    else:
                        shifts[a, c].push(s)
            for c in (-1, 0, 1):
                planes[Q_PLANE + c + 1, :, tile(t)] = jnp.where(row == 0, own[-1, c], jnp.where(row == 3, own[1, c], 0.0))
            planes[H_PLANE + 1, :, tile(t)] = jnp.where(row == 0, own[-1, 0], jnp.where(row == 3, own[1, 0], 0.0))
        if t >= 1:
            for c in (-1, 1):
                got = {}
                for a in (-1, 0, 1):
                    got[a] = shifts[a, c].take(t - 1)
                    planes[M_PLANE + 3 * (a + 1) + c + 1, :, tile(t - 1)] = got[a]
                planes[H_PLANE + c + 1, :, tile(t - 1)] = jnp.where(row == 0, got[-1], jnp.where(row == 3, got[1], 0.0))


def even_strip():
    return lax.axis_index("space") % 2 == 0


def pack_rows(plane, blocks, paired, crossed):
    for even in (True, False):
        to_below, to_above = (paired, crossed) if even else (crossed, paired)

        @pl.when(even_strip() == even)
        def _():
            for out, r in ((to_below, 3), (to_above, 0)):
                for f in range(FIELDS):
                    early, late = blocks(f)
                    out[plane + 3 * f, :, :] = early[r : r + 1, :]
                    out[plane + 3 * f + 1, :, :] = early[4 + r : 5 + r, :]
                    out[plane + 3 * f + 2, :, :] = late[r : r + 1, :]


def unpack_rows(paired, crossed, above, below):
    for even in (True, False):

        @pl.when(even_strip() == even)
        def _():
            below[...] = (paired if even else crossed)[...]
            above[...] = (crossed if even else paired)[...]


def edges_kernel(mine, got, cells, paired, crossed):
    for day in (0, 1):

        @pl.when(lax.axis_index("day") == day)
        def _():
            early, late = (mine, got) if day == 0 else (got, mine)
            pack_rows(0, lambda f: (early.at[f], late.at[f]), paired, crossed)

    for even in (True, False):

        @pl.when(even_strip() == even)
        def _():
            paired[9, :, :] = cells[0, 3:4, :] if even else cells[0, 0:1, :]
            crossed[9, :, :] = cells[0, 0:1, :] if even else cells[0, 3:4, :]


def apply_rows(planes, at, base, terms):
    sums = []
    for c in (0, 1, 2):
        total = planes[base + c, :, at] * terms[0]
        total = total + planes[base + 3 + c, :, at] * terms[1]
        total = total + planes[base + 6 + c, :, at] * terms[2]
        sums.append(total)
    return sums


def inside_kernel(stencil, mine, got, planes, pairs, moved, buffer, semaphores):
    fetch((stencil,), (buffer,), semaphores)
    coefficients(buffer, planes)
    day = lax.axis_index("day")
    tiles = mine.shape[-1] // LANES
    row = position(0) % 4
    first = day == 0
    for f in range(FIELDS + 1):
        for half in (0, 1):
            shifts = (Shift(1), Shift(-1))
            middle = []
            for t in range(tiles + 1):
                if t < tiles:
                    x, y = mine[f, :, tile(t)], got[f, :, tile(t)]
                    u = jnp.where(first, x, y) if half == 0 else jnp.where(first, y, x)
                    pairs[half, f, :, tile(t)] = u
                    if f < FIELDS:
                        up = jnp.where(row == 0, 0.0, rolled(u, 1, 0))
                        down = jnp.where(row == 3, 0.0, rolled(u, -1, 0))
                        left, centre, right = apply_rows(planes, tile(t), M_PLANE, (up, u, down))
                        shifts[0].push(left)
                        shifts[1].push(right)
                        middle.append(centre)
                if t >= 1 and f < FIELDS:
                    moved[half, f, :, tile(t - 1)] = middle[t - 1] + shifts[0].take(t - 1) + shifts[1].take(t - 1)


def placed(above, below, index, at):
    row = position(0)
    spread = lambda ref, k: jnp.broadcast_to(ref[k, :, at], (8, LANES))
    first, second = index
    out = jnp.where(row < 2, spread(above, first), spread(below, first))
    if second is not None:
        late = jnp.where(row < 6, spread(above, second), spread(below, second))
        out = jnp.where(row < 4, out, late)
    return out


def image_kernel(pairs, moved, planes, cells, came_paired, came_crossed, image, leaves, rims, paired, crossed, above, below):
    unpack_rows(came_paired, came_crossed, above, below)
    tiles = moved.shape[-1] // LANES
    row = position(0)
    low = row < 4
    @pl.loop(0, FIELDS)
    def _(f):
        incoming = [(Shift(1), Shift(-1)) for _ in (0, 1)]
        scatter = [(Shift(-1), Shift(1)) for _ in (0, 1)]
        leaving = [(Shift(-1), Shift(1)) for _ in (0, 1)]
        kept = {}
        for t in range(tiles + 2):
            if t < tiles:
                at = tile(t)
                for half in (0, 1):
                    rim = placed(above, below, (3 * f, 3 * f + 1) if half == 0 else (3 * f + 2, None), at)
                    rims[half, f, :, at] = rim
                    incoming[half][0].push(planes[H_PLANE, :, at] * rim)
                    kept["in", half, t] = planes[H_PLANE + 1, :, at] * rim
                    incoming[half][1].push(planes[H_PLANE + 2, :, at] * rim)
            if 1 <= t <= tiles:
                q = t - 1
                at = tile(q)
                m = [
                    moved[half, f, :, at] + kept.pop(("in", half, q)) + incoming[half][0].take(q) + incoming[half][1].take(q)
                    for half in (0, 1)
                ]
                before = (jnp.where(low, 0.0, rolled(m[0], 4, 0)), rolled(jnp.where(low, m[1], m[0]), 4, 0))
                for half in (0, 1):
                    u = pairs[half, f, :, at]
                    w = cells[1, :, at] * (u - before[half])
                    left, centre, right = apply_rows(planes, at, T_PLANE, (rolled(w, -1, 0), w, rolled(w, 1, 0)))
                    scatter[half][0].push(left)
                    scatter[half][1].push(right)
                    leaving[half][0].push(planes[Q_PLANE, :, at] * w)
                    leaving[half][1].push(planes[Q_PLANE + 2, :, at] * w)
                    kept[half, q] = (w + pairs[half, FIELDS, :, at] * u, centre, planes[Q_PLANE + 1, :, at] * w)
            if t >= 2:
                q = t - 2
                at = tile(q)
                s, out = [], []
                for half in (0, 1):
                    own, centre, edge = kept.pop((half, q))
                    s.append(centre + scatter[half][0].take(q) + scatter[half][1].take(q))
                    out.append(edge + leaving[half][0].take(q) + leaving[half][1].take(q))
                    kept["own", half] = own
                after = (rolled(jnp.where(low, s[1], s[0]), 4, 0), jnp.where(low, rolled(s[1], 4, 0), 0.0))
                leaves[0, f, :, at] = rolled(jnp.where(low, out[1], out[0]), 4, 0)
                leaves[1, f, :, at] = rolled(out[1], 4, 0)
                for half in (0, 1):
                    image[half, f, :, at] = cells[0, :, at] * (kept.pop(("own", half)) - after[half])

    pack_rows(0, lambda f: (image.at[0, f], image.at[1, f]), paired, crossed)
    pack_rows(9, lambda f: (leaves.at[0, f], leaves.at[1, f]), paired, crossed)


def sums_kernel(*refs):
    pairs, part, leaves, planes, cells, first_paired, first_crossed, came_paired, came_crossed = refs[:9]
    image, rims, swap, sums, sea_above, sea_below, above, below, kept_sums = refs[9:]
    unpack_rows(first_paired.at[9:10], first_crossed.at[9:10], sea_above, sea_below)
    unpack_rows(came_paired, came_crossed, above, below)
    day = lax.axis_index("day")
    tiles = part.shape[-1] // LANES
    row = position(0)
    low = row < 4
    edge = (row % 4 == 0) | (row % 4 == 3)
    @pl.loop(0, FIELDS)
    def _(f):
        shifts = [(Shift(1), Shift(-1)) for _ in (0, 1)]
        kept = {}
        totals = [None] * 4
        for t in range(tiles + 1):
            if t < tiles:
                at = tile(t)
                wet = cells[0, :, at]
                wet_rim = placed(sea_above, sea_below, (0, 0), at)
                for half in (0, 1):
                    days = (3 * f, 3 * f + 1) if half == 0 else (3 * f + 2, None)
                    late = tuple(None if k is None else 9 + k for k in days)
                    came = placed(above, below, late, at)
                    keep = edge if half == 0 else edge & low
                    z = part[half, f, :, at] - jnp.where(keep, wet * came, 0.0)
                    rim = placed(above, below, days, at) - wet_rim * leaves[half, f, :, at]
                    image[half, f, :, at] = z
                    rims[half, f, :, at] = rim
                    up = jnp.where(row % 4 == 0, rim, rolled(z, 1, 0))
                    down = jnp.where(row % 4 == 3, rim, rolled(z, -1, 0))
                    left, centre, right = apply_rows(planes, at, M_PLANE, (up, z, down))
                    shifts[half][0].push(left)
                    shifts[half][1].push(right)
                    kept[half, t] = (z, centre)
            if t >= 1:
                q = t - 1
                at = tile(q)
                z, m = [], []
                for half in (0, 1):
                    own, centre = kept.pop((half, q))
                    z.append(own)
                    m.append(centre + shifts[half][0].take(q) + shifts[half][1].take(q))
                before = (jnp.where(low, 0.0, rolled(m[0], 4, 0)), rolled(jnp.where(low, m[1], m[0]), 4, 0))
                terms = [0.0] * 4
                for half in (0, 1):
                    b = pairs[half, f, :, at]
                    gap = z[half] - before[half]
                    terms[0] = terms[0] + b * b
                    terms[1] = terms[1] + b * z[half]
                    terms[2] = terms[2] + z[half] * z[half]
                    terms[3] = terms[3] + (cells[1, :, at] * gap * gap + pairs[half, FIELDS, :, at] * z[half] * z[half])
                if q == 0:
                    terms = [jnp.where(day == 0, x, 0.0) for x in terms]
                elif q == tiles - 1:
                    terms = [jnp.where(day == 0, 0.0, x) for x in terms]
                totals = [x if y is None else x + y for x, y in zip(terms, totals)]
        for k, x in enumerate(totals):
            kept_sums[4 * f + k, :, :] = x

    lane = lax.broadcasted_iota(jnp.int32, (1, LANES), 1)
    line = jnp.zeros((1, LANES), F32)
    for k in range(4 * FIELDS):
        total = jnp.sum(jnp.sum(kept_sums[k, :, :], axis=0, keepdims=True), axis=1, keepdims=True)
        line = jnp.where(lane == k, total, line)
    for k in range(sums.shape[0]):
        sums[k, :, :] = line
    for which in (0, 1):

        @pl.when(day == which)
        def _():
            for t in range(tiles - 1):
                swap[t, :, :] = image[1 - which, 0, :, tile(t + which)]


def fit_kernel(sums, mine, give, pairs, image, theirs, side_rims, image_rims, posterior, fitted, mean, cells, ready, semaphores):
    day = lax.axis_index("day")
    tiles = mine.shape[-1] // LANES
    row = position(0)
    low = row < 4
    line = sums[0, :, :]
    for k in range(1, sums.shape[0]):
        line = line + sums[k, :, :]
    weights = []
    for f in range(FIELDS):
        m = [jnp.broadcast_to(line[:, k : k + 1], (8, LANES)) for k in range(4 * f, 4 * f + 4)]
        step = m[0] / m[1]
        norm_next = step * step * m[2] - m[0]
        grown = 1.0 + norm_next / m[0]
        curvature = grown * grown * m[1] - 2.0 * step * grown * m[2] + step * step * m[3]
        second = norm_next / curvature
        weights.append((step + second * grown, -second * step))

    def store(at, x):
        mean[0, :, at] = x[0:4]
        mean[1, :, at] = x[4:8]

    on_side, on_image = weights[0]
    for which in (0, 1):

        @pl.when(day == which)
        def _():
            for t in range(tiles - 1):
                here, there = which * (tiles - 1), (1 - which) * (tiles - 1)
                own = on_side * mine[0, :, tile(t + which)] + on_image * image[which, 0, :, tile(t + which)]
                store(tile(here + t), own)
                store(tile(there + t), on_side * give[0, :, tile(t + 1 - which)] + on_image * theirs[t, :, :])

    out_mean = pltpu.make_async_copy(mean, posterior, semaphores.at[0])
    out_mean.start()

    wide = {(f, half): (Shift(1), Shift(-1)) for f in (1, 2) for half in (0, 1)}
    kept = {}
    for t in range(tiles + 1):
        if t < tiles:
            at = tile(t)
            for f in (1, 2):
                on_side, on_image = weights[f]
                for half in (0, 1):
                    x = on_side * pairs[half, f, :, at] + on_image * image[half, f, :, at]
                    rim = on_side * side_rims[half, f, :, at] + on_image * image_rims[half, f, :, at]
                    up = jnp.where(row % 4 == 0, rim, rolled(x, 1, 0))
                    down = jnp.where(row % 4 == 3, rim, rolled(x, -1, 0))
                    box = x + up + down
                    wide[f, half][0].push(box)
                    wide[f, half][1].push(box)
                    kept[f, half, t] = (x, box)
        if t >= 1:
            q = t - 1
            totals = [0.0] * 5
            for f in (1, 2):
                (x0, box0), (x1, box1) = kept.pop((f, 0, q)), kept.pop((f, 1, q))
                targets = (rolled(jnp.where(low, x1, x0), 4, 0), rolled(x1, 4, 0))
                for half, (x, box) in enumerate(((x0, box0), (x1, box1))):
                    lap = box + wide[f, half][0].take(q) + wide[f, half][1].take(q) - 9.0 * x
                    if half == 1:
                        x, lap = jnp.where(low, x, 0.0), jnp.where(low, lap, 0.0)
                    target = targets[half]
                    for k, term in enumerate((x * x, x * lap, lap * lap, x * target, lap * target)):
                        totals[k] = totals[k] + term
            m = [x + rolled(x, 4, 0) for x in totals]
            first, second = m[0] + RIDGE, m[2] + RIDGE
            inverse = 1.0 / (first * second - m[1] * m[1])
            persistence = (second * m[3] - m[1] * m[4]) * inverse
            diffusion = (first * m[4] - m[1] * m[3]) * inverse

            cells[0, :, tile(q)] = persistence[0:4]
            cells[1, :, tile(q)] = diffusion[0:4]
    for which in (0, 1):

        @pl.when(day == which)
        def _():
            ready[...] = cells[:, :, which * LANES : which * LANES + ready.shape[-1]]

    out_fit = pltpu.make_async_copy(ready, fitted, semaphores.at[1])
    out_fit.start()
    out_mean.wait()
    out_fit.wait()


VMEM = pl.BlockSpec(memory_space=pltpu.VMEM)
HBM = pl.BlockSpec(memory_space=pltpu.HBM)


def call(kernel, outs, *args, scratch=(), source=None, target=VMEM, flops=2_000_000):
    size = sum(x.size * x.dtype.itemsize for x in args)
    return pl.pallas_call(
        kernel,
        out_shape=[jax.ShapeDtypeStruct(shape, F32) for shape in outs],
        in_specs=source or [VMEM] * len(args),
        out_specs=[target] * len(outs),
        scratch_shapes=scratch,
        cost_estimate=pl.CostEstimate(flops=flops, bytes_accessed=size, transcendentals=0),
        compiler_params=pltpu.CompilerParams(vmem_limit_bytes=32 << 20),
    )(*args)


def kept_in_hbm(*args):
    return tuple(pltpu.with_memory_space_constraint(x, pltpu.HBM) for x in args)


def buffers(*args):
    return [pltpu.VMEM(x.shape, x.dtype) for x in args] + [pltpu.SemaphoreType.DMA((len(args),))]


def shards(observed, gap_mask, sea_mask, stencil, precision, noise_precision, perturbation):
    cols = observed.shape[-1]
    devices = lax.axis_size("space") * lax.axis_size("day")
    half = cols // 2
    width = half + LANES
    pair = (8, width)
    row = (1, width)
    same = lambda s: s
    paired_space = lambda s: s ^ 1
    crossed_space = lambda s: ((s + 1) ^ 1) - 1

    raw = kept_in_hbm(observed, gap_mask, sea_mask, precision, noise_precision, perturbation)
    mine, give, cells = call(
        right_sides_kernel, [(4, *pair)] * 2 + [(2, *pair)], *raw, scratch=buffers(*raw), source=[HBM] * len(raw)
    )
    got = send(give, same, lambda d: 1 - d)
    paired, crossed = call(edges_kernel, [(10, *row)] * 2, mine, got, cells)
    first_paired = send(paired, paired_space)
    first_crossed = send(crossed, crossed_space)
    raw = kept_in_hbm(stencil)
    planes, pairs, moved = call(
        inside_kernel,
        [(PLANES, *pair), (2, 4, *pair), (2, 3, *pair)],
        *raw, mine, got,
        scratch=buffers(*raw),
        source=[HBM, VMEM, VMEM],
    )
    part, leaves, side_rims, paired, crossed = call(
        image_kernel,
        [(2, 3, *pair)] * 3 + [(18, *row)] * 2,
        pairs, moved, planes, cells, first_paired, first_crossed,
        scratch=[pltpu.VMEM((10, *row), F32)] * 2,
    )
    paired = send(paired, paired_space)
    crossed = send(crossed, crossed_space)
    image, image_rims, swap, sums = call(
        sums_kernel,
        [(2, 3, *pair), (2, 3, *pair), (half // LANES, 8, LANES), (devices, 1, LANES)],
        pairs, part, leaves, planes, cells, first_paired, first_crossed, paired, crossed,
        scratch=[pltpu.VMEM((1, *row), F32)] * 2 + [pltpu.VMEM((18, *row), F32)] * 2 + [pltpu.VMEM((4 * FIELDS, 8, LANES), F32)],
    )
    theirs = send(swap, same, lambda d: 1 - d)
    sums = lax.all_to_all(sums, ("space", "day"), 0, 0)
    fit = (2, observed.shape[1])
    posterior, fitted = call(
        fit_kernel,
        [observed.shape, (*fit, half)],
        sums, mine, give, pairs, image, theirs, side_rims, image_rims,
        scratch=[
            pltpu.VMEM(observed.shape, F32),
            pltpu.VMEM((*fit, width), F32),
            pltpu.VMEM((*fit, half), F32),
            pltpu.SemaphoreType.DMA((2,)),
        ],
        target=HBM,
    )
    return posterior, fitted


def solution(mesh):
    placed_args = (
        P("day", ("region", "space"), None),
        P("day", ("region", "space"), None),
        P(("region", "space"), None),
        P(None, ("region", "space"), None),
        P(("region", "space"), None),
        P(("region", "space"), None),
        P(None, "day", ("region", "space"), None),
    )
    return jax.shard_map(
        shards,
        mesh=mesh,
        in_specs=placed_args,
        out_specs=(P("day", ("region", "space"), None), P(None, ("region", "space"), "day")),
        check_vma=False,
    )
```

```python
import jax
import jax.numpy as jnp
from jax import lax
from jax.experimental import pallas as pl
from jax.experimental.pallas import tpu as pltpu
from jax.sharding import PartitionSpec as P

RIDGE = 1.0
LANES = 128
FIELDS = 3
F32 = jnp.float32

M_PLANE, H_PLANE, PLANES = 0, 9, 12


def send(x, space_of, day_of=lambda d: d):
    spaces, days = lax.axis_size("space"), lax.axis_size("day")
    pairs = []
    for s in range(spaces):
        for d in range(days):
            to_s, to_d = space_of(s), day_of(d)
            if 0 <= to_s < spaces:
                pairs.append((s * days + d, to_s * days + to_d))
    return lax.ppermute(x, ("space", "day"), pairs)


def position(axis):
    return lax.broadcasted_iota(jnp.int32, (8, LANES), axis)


def rolled(x, step, axis):
    return pltpu.roll(x, step % x.shape[axis], axis)


def tile(t):
    return pl.ds(t * LANES, LANES)


def dynamic_tile(start, t):
    return pl.ds(pl.multiple_of(start + t * LANES, LANES), LANES)


def doubled(x):
    return jnp.concatenate([x, x], 0)


class Shift:
    def __init__(self, step):
        self.step, self.edge, self.tiles = step, (0 if step > 0 else LANES - 1), []

    def push(self, x):
        self.tiles.append(rolled(x, self.step, 1))

    def take(self, t):
        beside = t - self.step
        here = self.tiles[t]
        other = self.tiles[beside] if 0 <= beside < len(self.tiles) else jnp.zeros_like(here)
        return jnp.where(position(1) == self.edge, other, here)


def fetch(sources, buffers, semaphores):
    copies = [pltpu.make_async_copy(x, y, semaphores.at[k]) for k, (x, y) in enumerate(zip(sources, buffers))]
    for copy in copies:
        copy.start()
    for copy in copies:
        copy.wait()


def right_sides_kernel(*refs):
    sources, (mine, give, cells), buffers, semaphores = refs[:6], refs[6:9], refs[9:15], refs[15]
    fetch(sources, buffers, semaphores)
    observed, gap, sea, precision, noise, perturbation = buffers
    day = lax.axis_index("day")
    tiles = mine.shape[-1] // LANES
    reach = observed.shape[-1] - mine.shape[-1]
    for out, side in ((mine, day), (give, 1 - day)):
        start = side * reach
        for t in range(tiles):
            at = dynamic_tile(start, t)
            both = lambda ref, *lead: jnp.concatenate([ref[(*lead, 0, slice(None), at)], ref[(*lead, 1, slice(None), at)]], 0)
            wet = doubled(sea[:, at].astype(F32))
            if out is mine:
                cells[0, :, tile(t)] = wet
                cells[1, :, tile(t)] = doubled(precision[:, at])
            seen = doubled(noise[:, at]) * both(gap).astype(F32)
            base = wet * seen * both(observed)
            spread = wet * jnp.sqrt(doubled(precision[:, at]) + seen)
            out[0, :, tile(t)] = base
            out[1, :, tile(t)] = base + spread * both(perturbation, 0).astype(F32)
            out[2, :, tile(t)] = base + spread * both(perturbation, 1).astype(F32)
            out[3, :, tile(t)] = seen


def coefficients(stencil, planes):
    width = planes.shape[-1]
    tiles = width // LANES
    start = lax.axis_index("day") * (stencil.shape[-1] - width)
    row = position(0) % 4
    shifts = {(a, c): Shift(c) for a in (-1, 0, 1) for c in (-1, 1)}
    middle = {}
    for t in range(tiles + 1):
        if t < tiles:
            at = dynamic_tile(start, t)
            for a in (-1, 0, 1):
                for c in (-1, 0, 1):
                    s = doubled(stencil[3 * (a + 1) + c + 1, :, at].astype(F32))
                    if c == 0:
                        middle[a, t] = s
                    else:
                        shifts[a, c].push(s)
        if t >= 1:
            for c in (-1, 0, 1):
                got = {a: shifts[a, c].take(t - 1) if c else middle.pop((a, t - 1)) for a in (-1, 0, 1)}
                for a in (-1, 0, 1):
                    planes[M_PLANE + 3 * (a + 1) + c + 1, :, tile(t - 1)] = got[a]
                planes[H_PLANE + c + 1, :, tile(t - 1)] = jnp.where(row == 0, got[-1], jnp.where(row == 3, got[1], 0.0))


def even_strip():
    return lax.axis_index("space") % 2 == 0


def pack_rows(plane, blocks, paired, crossed):
    for even in (True, False):
        to_below, to_above = (paired, crossed) if even else (crossed, paired)

        @pl.when(even_strip() == even)
        def _():
            for out, r in ((to_below, 3), (to_above, 0)):
                for f in range(FIELDS):
                    early, late = blocks(f)
                    out[plane + 3 * f, :, :] = early[r : r + 1, :]
                    out[plane + 3 * f + 1, :, :] = early[4 + r : 5 + r, :]
                    out[plane + 3 * f + 2, :, :] = late[r : r + 1, :]


def unpack_rows(paired, crossed, above, below):
    for even in (True, False):

        @pl.when(even_strip() == even)
        def _():
            below[...] = (paired if even else crossed)[...]
            above[...] = (crossed if even else paired)[...]


def edges_kernel(mine, got, cells, paired, crossed):
    for day in (0, 1):

        @pl.when(lax.axis_index("day") == day)
        def _():
            early, late = (mine, got) if day == 0 else (got, mine)
            pack_rows(0, lambda f: (early.at[f], late.at[f]), paired, crossed)

    for even in (True, False):

        @pl.when(even_strip() == even)
        def _():
            paired[9, :, :] = cells[0, 3:4, :] if even else cells[0, 0:1, :]
            crossed[9, :, :] = cells[0, 0:1, :] if even else cells[0, 3:4, :]


def apply_rows(planes, at, terms):
    sums = []
    for c in (0, 1, 2):
        total = planes[M_PLANE + c, :, at] * terms[0]
        total = total + planes[M_PLANE + 3 + c, :, at] * terms[1]
        total = total + planes[M_PLANE + 6 + c, :, at] * terms[2]
        sums.append(total)
    return sums


def apply_columns(planes, at, terms):
    sums = []
    for a in (0, 3, 6):
        total = planes[M_PLANE + a, :, at] * terms[0]
        total = total + planes[M_PLANE + a + 1, :, at] * terms[1]
        total = total + planes[M_PLANE + a + 2, :, at] * terms[2]
        sums.append(total)
    return sums


def inside_kernel(stencil, mine, got, planes, pairs, moved, buffer, semaphores):
    fetch((stencil,), (buffer,), semaphores)
    coefficients(buffer, planes)
    day = lax.axis_index("day")
    tiles = mine.shape[-1] // LANES
    row = position(0) % 4
    first = day == 0
    for f in range(FIELDS + 1):
        for half in (0, 1):
            shifts = (Shift(1), Shift(-1))
            middle = []
            for t in range(tiles + 1):
                if t < tiles:
                    x, y = mine[f, :, tile(t)], got[f, :, tile(t)]
                    u = jnp.where(first, x, y) if half == 0 else jnp.where(first, y, x)
                    pairs[half, f, :, tile(t)] = u
                    if f < FIELDS:
                        up = jnp.where(row == 0, 0.0, rolled(u, 1, 0))
                        down = jnp.where(row == 3, 0.0, rolled(u, -1, 0))
                        left, centre, right = apply_rows(planes, tile(t), (up, u, down))
                        shifts[0].push(left)
                        shifts[1].push(right)
                        middle.append(centre)
                if t >= 1 and f < FIELDS:
                    moved[half, f, :, tile(t - 1)] = middle[t - 1] + shifts[0].take(t - 1) + shifts[1].take(t - 1)


def placed(above, below, index, at):
    row = position(0)
    spread = lambda ref, k: jnp.broadcast_to(ref[k, :, at], (8, LANES))
    first, second = index
    out = jnp.where(row < 2, spread(above, first), spread(below, first))
    if second is not None:
        late = jnp.where(row < 6, spread(above, second), spread(below, second))
        out = jnp.where(row < 4, out, late)
    return out


def image_kernel(pairs, moved, planes, cells, came_paired, came_crossed, image, leaves, rims, paired, crossed, above, below):
    unpack_rows(came_paired, came_crossed, above, below)
    tiles = moved.shape[-1] // LANES
    row = position(0)
    low = row < 4
    edge = row % 4

    @pl.loop(0, FIELDS)
    def _(f):
        incoming = [(Shift(1), Shift(-1)) for _ in (0, 1)]
        beside = [(Shift(-1), Shift(1)) for _ in (0, 1)]
        kept = {}
        for t in range(tiles + 2):
            if t < tiles:
                at = tile(t)
                for half in (0, 1):
                    rim = placed(above, below, (3 * f, 3 * f + 1) if half == 0 else (3 * f + 2, None), at)
                    rims[half, f, :, at] = rim
                    incoming[half][0].push(planes[H_PLANE, :, at] * rim)
                    kept["in", half, t] = planes[H_PLANE + 1, :, at] * rim
                    incoming[half][1].push(planes[H_PLANE + 2, :, at] * rim)
            if 1 <= t <= tiles:
                q = t - 1
                at = tile(q)
                m = [
                    moved[half, f, :, at] + kept.pop(("in", half, q)) + incoming[half][0].take(q) + incoming[half][1].take(q)
                    for half in (0, 1)
                ]
                before = (jnp.where(low, 0.0, rolled(m[0], 4, 0)), rolled(jnp.where(low, m[1], m[0]), 4, 0))
                for half in (0, 1):
                    u = pairs[half, f, :, at]
                    w = cells[1, :, at] * (u - before[half])
                    beside[half][0].push(w)
                    beside[half][1].push(w)
                    kept[half, q] = (w, w + pairs[half, FIELDS, :, at] * u)
            if t >= 2:
                q = t - 2
                at = tile(q)
                s, out = [], []
                for half in (0, 1):
                    w, kept["own", half] = kept.pop((half, q))
                    up, stay, down = apply_columns(planes, at, (beside[half][0].take(q), w, beside[half][1].take(q)))
                    s.append(stay + jnp.where(edge == 3, 0.0, rolled(up, -1, 0)) + jnp.where(edge == 0, 0.0, rolled(down, 1, 0)))
                    out.append(jnp.where(edge == 0, up, down))
                after = (rolled(jnp.where(low, s[1], s[0]), 4, 0), jnp.where(low, rolled(s[1], 4, 0), 0.0))
                leaves[0, f, :, at] = rolled(jnp.where(low, out[1], out[0]), 4, 0)
                leaves[1, f, :, at] = rolled(out[1], 4, 0)
                for half in (0, 1):
                    image[half, f, :, at] = cells[0, :, at] * (kept.pop(("own", half)) - after[half])

    pack_rows(0, lambda f: (image.at[0, f], image.at[1, f]), paired, crossed)
    pack_rows(9, lambda f: (leaves.at[0, f], leaves.at[1, f]), paired, crossed)


def sums_kernel(*refs):
    pairs, part, leaves, planes, cells, first_paired, first_crossed, came_paired, came_crossed = refs[:9]
    image, rims, swap, sums, sea_above, sea_below, above, below, kept_sums = refs[9:]
    unpack_rows(first_paired.at[9:10], first_crossed.at[9:10], sea_above, sea_below)
    unpack_rows(came_paired, came_crossed, above, below)
    day = lax.axis_index("day")
    tiles = part.shape[-1] // LANES
    row = position(0)
    low = row < 4
    edge = (row % 4 == 0) | (row % 4 == 3)

    @pl.loop(0, FIELDS)
    def _(f):
        shifts = [(Shift(1), Shift(-1)) for _ in (0, 1)]
        kept = {}
        totals = [None] * 4
        for t in range(tiles + 1):
            if t < tiles:
                at = tile(t)
                wet = cells[0, :, at]
                wet_rim = placed(sea_above, sea_below, (0, 0), at)
                for half in (0, 1):
                    days = (3 * f, 3 * f + 1) if half == 0 else (3 * f + 2, None)
                    late = tuple(None if k is None else 9 + k for k in days)
                    came = placed(above, below, late, at)
                    keep = edge if half == 0 else edge & low
                    z = part[half, f, :, at] - jnp.where(keep, wet * came, 0.0)
                    rim = placed(above, below, days, at) - wet_rim * leaves[half, f, :, at]
                    image[half, f, :, at] = z
                    rims[half, f, :, at] = rim
                    up = jnp.where(row % 4 == 0, rim, rolled(z, 1, 0))
                    down = jnp.where(row % 4 == 3, rim, rolled(z, -1, 0))
                    left, centre, right = apply_rows(planes, at, (up, z, down))
                    shifts[half][0].push(left)
                    shifts[half][1].push(right)
                    kept[half, t] = (z, centre)
            if t >= 1:
                q = t - 1
                at = tile(q)
                z, m = [], []
                for half in (0, 1):
                    own, centre = kept.pop((half, q))
                    z.append(own)
                    m.append(centre + shifts[half][0].take(q) + shifts[half][1].take(q))
                before = (jnp.where(low, 0.0, rolled(m[0], 4, 0)), rolled(jnp.where(low, m[1], m[0]), 4, 0))
                terms = [0.0] * 4
                for half in (0, 1):
                    b = pairs[half, f, :, at]
                    gap = z[half] - before[half]
                    terms[0] = terms[0] + b * b
                    terms[1] = terms[1] + b * z[half]
                    terms[2] = terms[2] + z[half] * z[half]
                    terms[3] = terms[3] + (cells[1, :, at] * gap * gap + pairs[half, FIELDS, :, at] * z[half] * z[half])
                if q == 0:
                    terms = [jnp.where(day == 0, x, 0.0) for x in terms]
                elif q == tiles - 1:
                    terms = [jnp.where(day == 0, 0.0, x) for x in terms]
                totals = [x if y is None else x + y for x, y in zip(terms, totals)]
        for k, x in enumerate(totals):
            kept_sums[4 * f + k, :, :] = x

    lane = lax.broadcasted_iota(jnp.int32, (1, LANES), 1)
    line = jnp.zeros((1, LANES), F32)
    for k in range(4 * FIELDS):
        total = jnp.sum(jnp.sum(kept_sums[k, :, :], axis=0, keepdims=True), axis=1, keepdims=True)
        line = jnp.where(lane == k, total, line)
    for k in range(sums.shape[0]):
        sums[k, :, :] = line
    for which in (0, 1):

        @pl.when(day == which)
        def _():
            for t in range(tiles - 1):
                swap[t, :, :] = image[1 - which, 0, :, tile(t + which)]


def fit_kernel(sums, mine, give, pairs, image, theirs, side_rims, image_rims, posterior, fitted, mean, cells, ready, semaphores):
    day = lax.axis_index("day")
    tiles = mine.shape[-1] // LANES
    row = position(0)
    low = row < 4
    line = sums[0, :, :]
    for k in range(1, sums.shape[0]):
        line = line + sums[k, :, :]
    weights = []
    for f in range(FIELDS):
        m = [jnp.broadcast_to(line[:, k : k + 1], (8, LANES)) for k in range(4 * f, 4 * f + 4)]
        step = m[0] / m[1]
        norm_next = step * step * m[2] - m[0]
        grown = 1.0 + norm_next / m[0]
        curvature = grown * grown * m[1] - 2.0 * step * grown * m[2] + step * step * m[3]
        second = norm_next / curvature
        weights.append((step + second * grown, -second * step))

    def store(at, x):
        mean[0, :, at] = x[0:4]
        mean[1, :, at] = x[4:8]

    on_side, on_image = weights[0]
    for which in (0, 1):

        @pl.when(day == which)
        def _():
            for t in range(tiles - 1):
                here, there = which * (tiles - 1), (1 - which) * (tiles - 1)
                own = on_side * mine[0, :, tile(t + which)] + on_image * image[which, 0, :, tile(t + which)]
                store(tile(here + t), own)
                store(tile(there + t), on_side * give[0, :, tile(t + 1 - which)] + on_image * theirs[t, :, :])

    out_mean = pltpu.make_async_copy(mean, posterior, semaphores.at[0])
    out_mean.start()

    wide = {(f, half): (Shift(1), Shift(-1)) for f in (1, 2) for half in (0, 1)}
    kept = {}
    for t in range(tiles + 1):
        if t < tiles:
            at = tile(t)
            for f in (1, 2):
                on_side, on_image = weights[f]
                for half in (0, 1):
                    x = on_side * pairs[half, f, :, at] + on_image * image[half, f, :, at]
                    rim = on_side * side_rims[half, f, :, at] + on_image * image_rims[half, f, :, at]
                    up = jnp.where(row % 4 == 0, rim, rolled(x, 1, 0))
                    down = jnp.where(row % 4 == 3, rim, rolled(x, -1, 0))
                    box = x + up + down
                    wide[f, half][0].push(box)
                    wide[f, half][1].push(box)
                    kept[f, half, t] = (x, box)
        if t >= 1:
            q = t - 1
            totals = [0.0] * 5
            for f in (1, 2):
                (x0, box0), (x1, box1) = kept.pop((f, 0, q)), kept.pop((f, 1, q))
                targets = (rolled(jnp.where(low, x1, x0), 4, 0), rolled(x1, 4, 0))
                for half, (x, box) in enumerate(((x0, box0), (x1, box1))):
                    lap = box + wide[f, half][0].take(q) + wide[f, half][1].take(q) - 9.0 * x
                    if half == 1:
                        x, lap = jnp.where(low, x, 0.0), jnp.where(low, lap, 0.0)
                    target = targets[half]
                    for k, term in enumerate((x * x, x * lap, lap * lap, x * target, lap * target)):
                        totals[k] = totals[k] + term
            m = [x + rolled(x, 4, 0) for x in totals]
            first, second = m[0] + RIDGE, m[2] + RIDGE
            inverse = 1.0 / (first * second - m[1] * m[1])
            persistence = (second * m[3] - m[1] * m[4]) * inverse
            diffusion = (first * m[4] - m[1] * m[3]) * inverse

            cells[0, :, tile(q)] = persistence[0:4]
            cells[1, :, tile(q)] = diffusion[0:4]
    for which in (0, 1):

        @pl.when(day == which)
        def _():
            ready[...] = cells[:, :, which * LANES : which * LANES + ready.shape[-1]]

    out_fit = pltpu.make_async_copy(ready, fitted, semaphores.at[1])
    out_fit.start()
    out_mean.wait()
    out_fit.wait()


VMEM = pl.BlockSpec(memory_space=pltpu.VMEM)
HBM = pl.BlockSpec(memory_space=pltpu.HBM)


def call(kernel, outs, *args, scratch=(), source=None, target=VMEM, flops=2_000_000):
    size = sum(x.size * x.dtype.itemsize for x in args)
    return pl.pallas_call(
        kernel,
        out_shape=[jax.ShapeDtypeStruct(shape, F32) for shape in outs],
        in_specs=source or [VMEM] * len(args),
        out_specs=[target] * len(outs),
        scratch_shapes=scratch,
        cost_estimate=pl.CostEstimate(flops=flops, bytes_accessed=size, transcendentals=0),
        compiler_params=pltpu.CompilerParams(vmem_limit_bytes=32 << 20),
    )(*args)


def kept_in_hbm(*args):
    return tuple(pltpu.with_memory_space_constraint(x, pltpu.HBM) for x in args)


def buffers(*args):
    return [pltpu.VMEM(x.shape, x.dtype) for x in args] + [pltpu.SemaphoreType.DMA((len(args),))]


def shards(observed, gap_mask, sea_mask, stencil, precision, noise_precision, perturbation):
    cols = observed.shape[-1]
    devices = lax.axis_size("space") * lax.axis_size("day")
    half = cols // 2
    width = half + LANES
    pair = (8, width)
    row = (1, width)
    same = lambda s: s
    paired_space = lambda s: s ^ 1
    crossed_space = lambda s: ((s + 1) ^ 1) - 1

    raw = kept_in_hbm(observed, gap_mask, sea_mask, precision, noise_precision, perturbation)
    mine, give, cells = call(
        right_sides_kernel, [(4, *pair)] * 2 + [(2, *pair)], *raw, scratch=buffers(*raw), source=[HBM] * len(raw)
    )
    got = send(give, same, lambda d: 1 - d)
    paired, crossed = call(edges_kernel, [(10, *row)] * 2, mine, got, cells)
    first_paired = send(paired, paired_space)
    first_crossed = send(crossed, crossed_space)
    raw = kept_in_hbm(stencil)
    planes, pairs, moved = call(
        inside_kernel,
        [(PLANES, *pair), (2, 4, *pair), (2, 3, *pair)],
        *raw, mine, got,
        scratch=buffers(*raw),
        source=[HBM, VMEM, VMEM],
    )
    part, leaves, side_rims, paired, crossed = call(
        image_kernel,
        [(2, 3, *pair)] * 3 + [(18, *row)] * 2,
        pairs, moved, planes, cells, first_paired, first_crossed,
        scratch=[pltpu.VMEM((10, *row), F32)] * 2,
    )
    paired = send(paired, paired_space)
    crossed = send(crossed, crossed_space)
    image, image_rims, swap, sums = call(
        sums_kernel,
        [(2, 3, *pair), (2, 3, *pair), (half // LANES, 8, LANES), (devices, 1, LANES)],
        pairs, part, leaves, planes, cells, first_paired, first_crossed, paired, crossed,
        scratch=[pltpu.VMEM((1, *row), F32)] * 2 + [pltpu.VMEM((18, *row), F32)] * 2 + [pltpu.VMEM((4 * FIELDS, 8, LANES), F32)],
    )
    theirs = send(swap, same, lambda d: 1 - d)
    sums = lax.all_to_all(sums, ("space", "day"), 0, 0)
    fit = (2, observed.shape[1])
    posterior, fitted = call(
        fit_kernel,
        [observed.shape, (*fit, half)],
        sums, mine, give, pairs, image, theirs, side_rims, image_rims,
        scratch=[
            pltpu.VMEM(observed.shape, F32),
            pltpu.VMEM((*fit, width), F32),
            pltpu.VMEM((*fit, half), F32),
            pltpu.SemaphoreType.DMA((2,)),
        ],
        target=HBM,
    )
    return posterior, fitted


def solution(mesh):
    placed_args = (
        P("day", ("region", "space"), None),
        P("day", ("region", "space"), None),
        P(("region", "space"), None),
        P(None, ("region", "space"), None),
        P(("region", "space"), None),
        P(("region", "space"), None),
        P(None, "day", ("region", "space"), None),
    )
    return jax.shard_map(
        shards,
        mesh=mesh,
        in_specs=placed_args,
        out_specs=(P("day", ("region", "space"), None), P(None, ("region", "space"), "day")),
        check_vma=False,
    )
```

```python
import jax
import jax.numpy as jnp
from jax import lax
from jax.experimental import pallas as pl
from jax.experimental.pallas import tpu as pltpu
from jax.sharding import PartitionSpec as P

RIDGE = 1.0
LANES = 128
FIELDS = 3
F32 = jnp.float32

M_PLANE, H_PLANE, PLANES = 0, 9, 12


def send(x, space_of, day_of=lambda d: d):
    spaces, days = lax.axis_size("space"), lax.axis_size("day")
    pairs = []
    for s in range(spaces):
        for d in range(days):
            to_s, to_d = space_of(s), day_of(d)
            if 0 <= to_s < spaces:
                pairs.append((s * days + d, to_s * days + to_d))
    return lax.ppermute(x, ("space", "day"), pairs)


def position(axis):
    return lax.broadcasted_iota(jnp.int32, (8, LANES), axis)


def rolled(x, step, axis):
    return pltpu.roll(x, step % x.shape[axis], axis)


def tile(t):
    return pl.ds(t * LANES, LANES)


def dynamic_tile(start, t):
    return pl.ds(pl.multiple_of(start + t * LANES, LANES), LANES)


def doubled(x):
    return jnp.concatenate([x, x], 0)


class Shift:
    def __init__(self, step):
        self.step, self.edge, self.tiles = step, (0 if step > 0 else LANES - 1), []

    def push(self, x):
        self.tiles.append(rolled(x, self.step, 1))

    def take(self, t):
        beside = t - self.step
        here = self.tiles[t]
        other = self.tiles[beside] if 0 <= beside < len(self.tiles) else jnp.zeros_like(here)
        return jnp.where(position(1) == self.edge, other, here)


def fetch(sources, buffers, semaphores):
    copies = [pltpu.make_async_copy(x, y, semaphores.at[k]) for k, (x, y) in enumerate(zip(sources, buffers))]
    for copy in copies:
        copy.start()
    for copy in copies:
        copy.wait()


def right_sides_kernel(*refs):
    sources, (mine, give, cells), buffers, semaphores = refs[:6], refs[6:9], refs[9:15], refs[15]
    fetch(sources, buffers, semaphores)
    observed, gap, sea, precision, noise, perturbation = buffers
    day = lax.axis_index("day")
    tiles = mine.shape[-1] // LANES
    reach = observed.shape[-1] - mine.shape[-1]
    for out, side in ((mine, day), (give, 1 - day)):
        start = side * reach
        for t in range(tiles):
            at = dynamic_tile(start, t)
            both = lambda ref, *lead: jnp.concatenate([ref[(*lead, 0, slice(None), at)], ref[(*lead, 1, slice(None), at)]], 0)
            wet = doubled(sea[:, at].astype(F32))
            if out is mine:
                cells[0, :, tile(t)] = wet
                cells[1, :, tile(t)] = doubled(precision[:, at])
            seen = doubled(noise[:, at]) * both(gap).astype(F32)
            base = wet * seen * both(observed)
            spread = wet * jnp.sqrt(doubled(precision[:, at]) + seen)
            out[0, :, tile(t)] = base
            out[1, :, tile(t)] = base + spread * both(perturbation, 0).astype(F32)
            out[2, :, tile(t)] = base + spread * both(perturbation, 1).astype(F32)
            out[3, :, tile(t)] = seen


def coefficients(stencil, planes):
    width = planes.shape[-1]
    tiles = width // LANES
    start = lax.axis_index("day") * (stencil.shape[-1] - width)
    row = position(0) % 4
    shifts = {(a, c): Shift(c) for a in (-1, 0, 1) for c in (-1, 1)}
    middle = {}
    for t in range(tiles + 1):
        if t < tiles:
            at = dynamic_tile(start, t)
            for a in (-1, 0, 1):
                for c in (-1, 0, 1):
                    s = doubled(stencil[3 * (a + 1) + c + 1, :, at].astype(F32))
                    if c == 0:
                        middle[a, t] = s
                    else:
                        shifts[a, c].push(s)
        if t >= 1:
            for c in (-1, 0, 1):
                got = {a: shifts[a, c].take(t - 1) if c else middle.pop((a, t - 1)) for a in (-1, 0, 1)}
                for a in (-1, 0, 1):
                    planes[M_PLANE + 3 * (a + 1) + c + 1, :, tile(t - 1)] = got[a]
                planes[H_PLANE + c + 1, :, tile(t - 1)] = jnp.where(row == 0, got[-1], jnp.where(row == 3, got[1], 0.0))


def even_strip():
    return lax.axis_index("space") % 2 == 0


def pack_rows(plane, blocks, paired, crossed):
    for even in (True, False):
        to_below, to_above = (paired, crossed) if even else (crossed, paired)

        @pl.when(even_strip() == even)
        def _():
            for out, r in ((to_below, 3), (to_above, 0)):
                for f in range(FIELDS):
                    early, late = blocks(f)
                    out[plane + 3 * f, :, :] = early[r : r + 1, :]
                    out[plane + 3 * f + 1, :, :] = early[4 + r : 5 + r, :]
                    out[plane + 3 * f + 2, :, :] = late[r : r + 1, :]


def unpack_rows(paired, crossed, above, below):
    for even in (True, False):

        @pl.when(even_strip() == even)
        def _():
            below[...] = (paired if even else crossed)[...]
            above[...] = (crossed if even else paired)[...]


def edges_kernel(mine, got, cells, paired, crossed):
    for day in (0, 1):

        @pl.when(lax.axis_index("day") == day)
        def _():
            early, late = (mine, got) if day == 0 else (got, mine)
            pack_rows(0, lambda f: (early.at[f], late.at[f]), paired, crossed)

    for even in (True, False):

        @pl.when(even_strip() == even)
        def _():
            paired[9, :, :] = cells[0, 3:4, :] if even else cells[0, 0:1, :]
            crossed[9, :, :] = cells[0, 0:1, :] if even else cells[0, 3:4, :]


def apply_rows(planes, at, terms):
    sums = []
    for c in (0, 1, 2):
        total = planes[M_PLANE + c, :, at] * terms[0]
        total = total + planes[M_PLANE + 3 + c, :, at] * terms[1]
        total = total + planes[M_PLANE + 6 + c, :, at] * terms[2]
        sums.append(total)
    return sums


def apply_columns(planes, at, terms):
    sums = []
    for a in (0, 3, 6):
        total = planes[M_PLANE + a, :, at] * terms[0]
        total = total + planes[M_PLANE + a + 1, :, at] * terms[1]
        total = total + planes[M_PLANE + a + 2, :, at] * terms[2]
        sums.append(total)
    return sums


def inside_kernel(stencil, mine, got, planes, pairs, moved, buffer, semaphores):
    fetch((stencil,), (buffer,), semaphores)
    coefficients(buffer, planes)
    day = lax.axis_index("day")
    tiles = mine.shape[-1] // LANES
    row = position(0) % 4
    first = day == 0
    for f in range(FIELDS + 1):
        for half in (0, 1):
            shifts = (Shift(1), Shift(-1))
            middle = []
            for t in range(tiles + 1):
                if t < tiles:
                    x, y = mine[f, :, tile(t)], got[f, :, tile(t)]
                    u = jnp.where(first, x, y) if half == 0 else jnp.where(first, y, x)
                    pairs[half, f, :, tile(t)] = u
                    if f < FIELDS:
                        up = jnp.where(row == 0, 0.0, rolled(u, 1, 0))
                        down = jnp.where(row == 3, 0.0, rolled(u, -1, 0))
                        left, centre, right = apply_rows(planes, tile(t), (up, u, down))
                        shifts[0].push(left)
                        shifts[1].push(right)
                        middle.append(centre)
                if t >= 1 and f < FIELDS:
                    moved[half, f, :, tile(t - 1)] = middle[t - 1] + shifts[0].take(t - 1) + shifts[1].take(t - 1)


def placed(above, below, index, at):
    row = position(0)
    spread = lambda ref, k: jnp.broadcast_to(ref[k, :, at], (8, LANES))
    first, second = index
    out = jnp.where(row < 2, spread(above, first), spread(below, first))
    if second is not None:
        late = jnp.where(row < 6, spread(above, second), spread(below, second))
        out = jnp.where(row < 4, out, late)
    return out


def total(x):
    return jnp.sum(jnp.sum(x, axis=0, keepdims=True), axis=1, keepdims=True)


def image_kernel(*refs):
    pairs, moved, planes, cells, came_paired, came_crossed = refs[:6]
    image, leaves, rims, gaps, centres, paired, crossed, above, below = refs[6:]
    unpack_rows(came_paired, came_crossed, above, below)
    tiles = moved.shape[-1] // LANES
    row = position(0)
    low = row < 4
    edge = row % 4

    @pl.loop(0, FIELDS)
    def _(f):
        incoming = [(Shift(1), Shift(-1)) for _ in (0, 1)]
        beside = [(Shift(-1), Shift(1)) for _ in (0, 1)]
        kept = {}
        along = square = jnp.zeros((8, LANES), F32)
        for t in range(tiles + 2):
            if t < tiles:
                at = tile(t)
                for half in (0, 1):
                    rim = placed(above, below, (3 * f, 3 * f + 1) if half == 0 else (3 * f + 2, None), at)
                    rims[half, f, :, at] = rim
                    incoming[half][0].push(planes[H_PLANE, :, at] * rim)
                    kept["in", half, t] = planes[H_PLANE + 1, :, at] * rim
                    incoming[half][1].push(planes[H_PLANE + 2, :, at] * rim)
            if 1 <= t <= tiles:
                q = t - 1
                at = tile(q)
                m = [
                    moved[half, f, :, at] + kept.pop(("in", half, q)) + incoming[half][0].take(q) + incoming[half][1].take(q)
                    for half in (0, 1)
                ]
                before = (jnp.where(low, 0.0, rolled(m[0], 4, 0)), rolled(jnp.where(low, m[1], m[0]), 4, 0))
                for half in (0, 1):
                    u = pairs[half, f, :, at]
                    gap = u - before[half]
                    gaps[half, f, :, at] = gap
                    w = cells[1, :, at] * gap
                    beside[half][0].push(w)
                    beside[half][1].push(w)
                    kept[half, q] = (w, w + pairs[half, FIELDS, :, at] * u)
            if t >= 2:
                q = t - 2
                at = tile(q)
                s, out = [], []
                for half in (0, 1):
                    w, kept["own", half] = kept.pop((half, q))
                    up, stay, down = apply_columns(planes, at, (beside[half][0].take(q), w, beside[half][1].take(q)))
                    s.append(stay + jnp.where(edge == 3, 0.0, rolled(up, -1, 0)) + jnp.where(edge == 0, 0.0, rolled(down, 1, 0)))
                    out.append(jnp.where(edge == 0, up, down))
                after = (rolled(jnp.where(low, s[1], s[0]), 4, 0), jnp.where(low, rolled(s[1], 4, 0), 0.0))
                leaves[0, f, :, at] = rolled(jnp.where(low, out[1], out[0]), 4, 0)
                leaves[1, f, :, at] = rolled(out[1], 4, 0)
                for half in (0, 1):
                    z = cells[0, :, at] * (kept.pop(("own", half)) - after[half])
                    image[half, f, :, at] = z
                    u = pairs[half, f, :, at]
                    along = along + u * z
                    square = square + u * u
        along, square = total(along), total(square)
        centre = jnp.where(square > 0.0, along / jnp.where(square > 0.0, square, 1.0), 0.0)
        centres[f, :, :] = jnp.broadcast_to(centre, (8, LANES))

    pack_rows(0, lambda f: (image.at[0, f], image.at[1, f]), paired, crossed)
    pack_rows(9, lambda f: (leaves.at[0, f], leaves.at[1, f]), paired, crossed)


def sums_kernel(*refs):
    pairs, part, leaves, gaps, centres, planes, cells = refs[:7]
    first_paired, first_crossed, came_paired, came_crossed = refs[7:11]
    image, rims, swap, sums, sea_above, sea_below, above, below, kept_sums = refs[11:]
    unpack_rows(first_paired.at[9:10], first_crossed.at[9:10], sea_above, sea_below)
    unpack_rows(came_paired, came_crossed, above, below)
    day = lax.axis_index("day")
    tiles = part.shape[-1] // LANES
    row = position(0)
    low = row < 4
    edge = (row % 4 == 0) | (row % 4 == 3)

    @pl.loop(0, FIELDS)
    def _(f):
        shifts = [(Shift(1), Shift(-1)) for _ in (0, 1)]
        kept = {}
        totals = [None] * 6
        ratio = centres[f, :, :]
        for t in range(tiles + 1):
            if t < tiles:
                at = tile(t)
                wet = cells[0, :, at]
                wet_rim = placed(sea_above, sea_below, (0, 0), at)
                for half in (0, 1):
                    days = (3 * f, 3 * f + 1) if half == 0 else (3 * f + 2, None)
                    late = tuple(None if k is None else 9 + k for k in days)
                    came = placed(above, below, late, at)
                    keep = edge if half == 0 else edge & low
                    z = part[half, f, :, at] - jnp.where(keep, wet * came, 0.0)
                    rim = placed(above, below, days, at) - wet_rim * leaves[half, f, :, at]
                    image[half, f, :, at] = z
                    rims[half, f, :, at] = rim
                    up = jnp.where(row % 4 == 0, rim, rolled(z, 1, 0))
                    down = jnp.where(row % 4 == 3, rim, rolled(z, -1, 0))
                    left, centre, right = apply_rows(planes, at, (up, z, down))
                    shifts[half][0].push(left)
                    shifts[half][1].push(right)
                    kept[half, t] = (z, centre)
            if t >= 1:
                q = t - 1
                at = tile(q)
                z, m = [], []
                for half in (0, 1):
                    own, centre = kept.pop((half, q))
                    z.append(own)
                    m.append(centre + shifts[half][0].take(q) + shifts[half][1].take(q))
                before = (jnp.where(low, 0.0, rolled(m[0], 4, 0)), rolled(jnp.where(low, m[1], m[0]), 4, 0))
                terms = [0.0] * 6
                for half in (0, 1):
                    b = pairs[half, f, :, at]
                    y = z[half] - ratio * b
                    seen, gap = pairs[half, FIELDS, :, at], gaps[half, f, :, at]
                    weighted = cells[1, :, at] * gap
                    beside = (z[half] - before[half]) - ratio * gap
                    products = (
                        b * b,
                        b * y,
                        y * y,
                        weighted * gap + seen * b * b,
                        weighted * beside + seen * b * y,
                        cells[1, :, at] * beside * beside + seen * y * y,
                    )
                    terms = [x + product for x, product in zip(terms, products)]
                if q == 0:
                    terms = [jnp.where(day == 0, x, 0.0) for x in terms]
                elif q == tiles - 1:
                    terms = [jnp.where(day == 0, 0.0, x) for x in terms]
                totals = [x if y is None else x + y for x, y in zip(terms, totals)]
        for k, x in enumerate(totals):
            kept_sums[3 * k + f, :, :] = x

    lane = lax.broadcasted_iota(jnp.int32, (1, LANES), 1)
    line = jnp.zeros((1, LANES), F32)
    for k in range(6 * FIELDS):
        line = jnp.where(lane == k, total(kept_sums[k, :, :]), line)
    for f in range(FIELDS):
        line = jnp.where(lane == 6 * FIELDS + f, centres[f, 0:1, :], line)
    for k in range(sums.shape[0]):
        sums[k, :, :] = line
    for which in (0, 1):

        @pl.when(day == which)
        def _():
            for t in range(tiles - 1):
                swap[t, :, :] = image[1 - which, 0, :, tile(t + which)]


def fit_kernel(sums, mine, give, pairs, image, theirs, side_rims, image_rims, posterior, fitted, mean, cells, ready, lines, semaphores):
    day = lax.axis_index("day")
    tiles = mine.shape[-1] // LANES
    row = position(0)
    low = row < 4
    for k in range(sums.shape[0]):
        lines[k : k + 1, :] = sums[k, :, :]
    own = [lines[...]] + [rolled(lines[...], -3 * k, 1) for k in range(1, 7)]
    side_side, side_off, off_off, side_energy, cross_energy, off_energy, centre = own
    add = lambda x: jnp.sum(x, axis=0, keepdims=True)
    norm = add(side_side)
    ratio = add(centre * side_side + side_off) / norm
    move = ratio - centre
    off_norm = add(off_off - 2.0 * move * side_off + move * move * side_side)
    off_energy = add(off_energy - 2.0 * move * cross_energy + move * move * side_energy)
    cross_energy = add(cross_energy - move * side_energy)
    step = 1.0 / ratio
    norm_next = step * step * off_norm
    grown = norm_next / norm
    curvature = step * step * off_energy - 2.0 * step * grown * cross_energy + grown * grown * add(side_energy)
    second = norm_next / curvature
    on_both = (step + second * (1.0 + grown), -second * step)
    weights = [[jnp.broadcast_to(x[:, f : f + 1], (8, LANES)) for x in on_both] for f in range(FIELDS)]

    def store(at, x):
        mean[0, :, at] = x[0:4]
        mean[1, :, at] = x[4:8]

    on_side, on_image = weights[0]
    for which in (0, 1):

        @pl.when(day == which)
        def _():
            for t in range(tiles - 1):
                here, there = which * (tiles - 1), (1 - which) * (tiles - 1)
                own = on_side * mine[0, :, tile(t + which)] + on_image * image[which, 0, :, tile(t + which)]
                store(tile(here + t), own)
                store(tile(there + t), on_side * give[0, :, tile(t + 1 - which)] + on_image * theirs[t, :, :])

    out_mean = pltpu.make_async_copy(mean, posterior, semaphores.at[0])
    out_mean.start()

    wide = {(f, half): (Shift(1), Shift(-1)) for f in (1, 2) for half in (0, 1)}
    kept = {}
    for t in range(tiles + 1):
        if t < tiles:
            at = tile(t)
            for f in (1, 2):
                on_side, on_image = weights[f]
                for half in (0, 1):
                    x = on_side * pairs[half, f, :, at] + on_image * image[half, f, :, at]
                    rim = on_side * side_rims[half, f, :, at] + on_image * image_rims[half, f, :, at]
                    up = jnp.where(row % 4 == 0, rim, rolled(x, 1, 0))
                    down = jnp.where(row % 4 == 3, rim, rolled(x, -1, 0))
                    box = x + up + down
                    wide[f, half][0].push(box)
                    wide[f, half][1].push(box)
                    kept[f, half, t] = (x, box)
        if t >= 1:
            q = t - 1
            totals = [0.0] * 5
            for f in (1, 2):
                (x0, box0), (x1, box1) = kept.pop((f, 0, q)), kept.pop((f, 1, q))
                targets = (rolled(jnp.where(low, x1, x0), 4, 0), rolled(x1, 4, 0))
                for half, (x, box) in enumerate(((x0, box0), (x1, box1))):
                    lap = box + wide[f, half][0].take(q) + wide[f, half][1].take(q) - 9.0 * x
                    if half == 1:
                        x, lap = jnp.where(low, x, 0.0), jnp.where(low, lap, 0.0)
                    target = targets[half]
                    for k, term in enumerate((x * x, x * lap, lap * lap, x * target, lap * target)):
                        totals[k] = totals[k] + term
            m = [x + rolled(x, 4, 0) for x in totals]
            first, second = m[0] + RIDGE, m[2] + RIDGE
            inverse = 1.0 / (first * second - m[1] * m[1])
            persistence = (second * m[3] - m[1] * m[4]) * inverse
            diffusion = (first * m[4] - m[1] * m[3]) * inverse

            cells[0, :, tile(q)] = persistence[0:4]
            cells[1, :, tile(q)] = diffusion[0:4]
    for which in (0, 1):

        @pl.when(day == which)
        def _():
            ready[...] = cells[:, :, which * LANES : which * LANES + ready.shape[-1]]

    out_fit = pltpu.make_async_copy(ready, fitted, semaphores.at[1])
    out_fit.start()
    out_mean.wait()
    out_fit.wait()


VMEM = pl.BlockSpec(memory_space=pltpu.VMEM)
HBM = pl.BlockSpec(memory_space=pltpu.HBM)


def call(kernel, outs, *args, scratch=(), source=None, target=VMEM, flops=2_000_000):
    size = sum(x.size * x.dtype.itemsize for x in args)
    return pl.pallas_call(
        kernel,
        out_shape=[jax.ShapeDtypeStruct(shape, F32) for shape in outs],
        in_specs=source or [VMEM] * len(args),
        out_specs=[target] * len(outs),
        scratch_shapes=scratch,
        cost_estimate=pl.CostEstimate(flops=flops, bytes_accessed=size, transcendentals=0),
        compiler_params=pltpu.CompilerParams(vmem_limit_bytes=32 << 20),
    )(*args)


def kept_in_hbm(*args):
    return tuple(pltpu.with_memory_space_constraint(x, pltpu.HBM) for x in args)


def buffers(*args):
    return [pltpu.VMEM(x.shape, x.dtype) for x in args] + [pltpu.SemaphoreType.DMA((len(args),))]


def shards(observed, gap_mask, sea_mask, stencil, precision, noise_precision, perturbation):
    cols = observed.shape[-1]
    devices = lax.axis_size("space") * lax.axis_size("day")
    half = cols // 2
    width = half + LANES
    pair = (8, width)
    row = (1, width)
    same = lambda s: s
    paired_space = lambda s: s ^ 1
    crossed_space = lambda s: ((s + 1) ^ 1) - 1

    raw = kept_in_hbm(observed, gap_mask, sea_mask, precision, noise_precision, perturbation)
    mine, give, cells = call(
        right_sides_kernel, [(4, *pair)] * 2 + [(2, *pair)], *raw, scratch=buffers(*raw), source=[HBM] * len(raw)
    )
    got = send(give, same, lambda d: 1 - d)
    paired, crossed = call(edges_kernel, [(10, *row)] * 2, mine, got, cells)
    first_paired = send(paired, paired_space)
    first_crossed = send(crossed, crossed_space)
    raw = kept_in_hbm(stencil)
    planes, pairs, moved = call(
        inside_kernel,
        [(PLANES, *pair), (2, 4, *pair), (2, 3, *pair)],
        *raw, mine, got,
        scratch=buffers(*raw),
        source=[HBM, VMEM, VMEM],
    )
    part, leaves, side_rims, gaps, centres, paired, crossed = call(
        image_kernel,
        [(2, 3, *pair)] * 4 + [(FIELDS, 8, LANES)] + [(18, *row)] * 2,
        pairs, moved, planes, cells, first_paired, first_crossed,
        scratch=[pltpu.VMEM((10, *row), F32)] * 2,
    )
    paired = send(paired, paired_space)
    crossed = send(crossed, crossed_space)
    image, image_rims, swap, sums = call(
        sums_kernel,
        [(2, 3, *pair), (2, 3, *pair), (half // LANES, 8, LANES), (devices, 1, LANES)],
        pairs, part, leaves, gaps, centres, planes, cells, first_paired, first_crossed, paired, crossed,
        scratch=[pltpu.VMEM((1, *row), F32)] * 2 + [pltpu.VMEM((18, *row), F32)] * 2 + [pltpu.VMEM((6 * FIELDS, 8, LANES), F32)],
    )
    theirs = send(swap, same, lambda d: 1 - d)
    sums = lax.all_to_all(sums, ("space", "day"), 0, 0)
    fit = (2, observed.shape[1])
    posterior, fitted = call(
        fit_kernel,
        [observed.shape, (*fit, half)],
        sums, mine, give, pairs, image, theirs, side_rims, image_rims,
        scratch=[
            pltpu.VMEM(observed.shape, F32),
            pltpu.VMEM((*fit, width), F32),
            pltpu.VMEM((*fit, half), F32),
            pltpu.VMEM((devices, LANES), F32),
            pltpu.SemaphoreType.DMA((2,)),
        ],
        target=HBM,
    )
    return posterior, fitted


def solution(mesh):
    placed_args = (
        P("day", ("region", "space"), None),
        P("day", ("region", "space"), None),
        P(("region", "space"), None),
        P(None, ("region", "space"), None),
        P(("region", "space"), None),
        P(("region", "space"), None),
        P(None, "day", ("region", "space"), None),
    )
    return jax.shard_map(
        shards,
        mesh=mesh,
        in_specs=placed_args,
        out_specs=(P("day", ("region", "space"), None), P(None, ("region", "space"), "day")),
        check_vma=False,
    )
```

```python
import jax
import jax.numpy as jnp
from jax import lax
from jax.experimental import pallas as pl
from jax.experimental.pallas import tpu as pltpu
from jax.sharding import PartitionSpec as P

RIDGE = 1.0
LANES = 128
FIELDS = 3
F32 = jnp.float32

M_PLANE, H_PLANE, PLANES = 0, 9, 12


def send(x, space_of, day_of=lambda d: d):
    spaces, days = lax.axis_size("space"), lax.axis_size("day")
    pairs = []
    for s in range(spaces):
        for d in range(days):
            to_s, to_d = space_of(s), day_of(d)
            if 0 <= to_s < spaces:
                pairs.append((s * days + d, to_s * days + to_d))
    return lax.ppermute(x, ("space", "day"), pairs)


def position(axis):
    return lax.broadcasted_iota(jnp.int32, (8, LANES), axis)


def rolled(x, step, axis):
    return pltpu.roll(x, step % x.shape[axis], axis)


def tile(t):
    return pl.ds(t * LANES, LANES)


def dynamic_tile(start, t):
    return pl.ds(pl.multiple_of(start + t * LANES, LANES), LANES)


def doubled(x):
    return jnp.concatenate([x, x], 0)


class Shift:
    def __init__(self, step):
        self.step, self.edge, self.tiles = step, (0 if step > 0 else LANES - 1), []

    def push(self, x):
        self.tiles.append(rolled(x, self.step, 1))

    def take(self, t):
        beside = t - self.step
        here = self.tiles[t]
        other = self.tiles[beside] if 0 <= beside < len(self.tiles) else jnp.zeros_like(here)
        return jnp.where(position(1) == self.edge, other, here)


def fetch(sources, buffers, semaphores):
    copies = [pltpu.make_async_copy(x, y, semaphores.at[k]) for k, (x, y) in enumerate(zip(sources, buffers))]
    for copy in copies:
        copy.start()
    for copy in copies:
        copy.wait()


def right_sides_kernel(*refs):
    sources, (mine, give, cells), buffers, semaphores = refs[:6], refs[6:9], refs[9:15], refs[15]
    fetch(sources, buffers, semaphores)
    observed, gap, sea, precision, noise, perturbation = buffers
    day = lax.axis_index("day")
    tiles = mine.shape[-1] // LANES
    reach = observed.shape[-1] - mine.shape[-1]
    for out, side in ((mine, day), (give, 1 - day)):
        start = side * reach
        for t in range(tiles):
            at = dynamic_tile(start, t)
            both = lambda ref, *lead: jnp.concatenate([ref[(*lead, 0, slice(None), at)], ref[(*lead, 1, slice(None), at)]], 0)
            wet = doubled(sea[:, at].astype(F32))
            if out is mine:
                cells[0, :, tile(t)] = wet
                cells[1, :, tile(t)] = doubled(precision[:, at])
            seen = doubled(noise[:, at]) * both(gap).astype(F32)
            base = wet * seen * both(observed)
            spread = wet * jnp.sqrt(doubled(precision[:, at]) + seen)
            out[0, :, tile(t)] = base
            out[1, :, tile(t)] = base + spread * both(perturbation, 0).astype(F32)
            out[2, :, tile(t)] = base + spread * both(perturbation, 1).astype(F32)
            out[3, :, tile(t)] = seen


def coefficients(stencil, planes):
    width = planes.shape[-1]
    tiles = width // LANES
    start = lax.axis_index("day") * (stencil.shape[-1] - width)
    row = position(0) % 4
    shifts = {(a, c): Shift(c) for a in (-1, 0, 1) for c in (-1, 1)}
    middle = {}
    for t in range(tiles + 1):
        if t < tiles:
            at = dynamic_tile(start, t)
            for a in (-1, 0, 1):
                for c in (-1, 0, 1):
                    s = doubled(stencil[3 * (a + 1) + c + 1, :, at].astype(F32))
                    if c == 0:
                        middle[a, t] = s
                    else:
                        shifts[a, c].push(s)
        if t >= 1:
            for c in (-1, 0, 1):
                got = {a: shifts[a, c].take(t - 1) if c else middle.pop((a, t - 1)) for a in (-1, 0, 1)}
                for a in (-1, 0, 1):
                    planes[M_PLANE + 3 * (a + 1) + c + 1, :, tile(t - 1)] = got[a]
                planes[H_PLANE + c + 1, :, tile(t - 1)] = jnp.where(row == 0, got[-1], jnp.where(row == 3, got[1], 0.0))


def even_strip():
    return lax.axis_index("space") % 2 == 0


def pack_rows(plane, blocks, paired, crossed):
    for even in (True, False):
        to_below, to_above = (paired, crossed) if even else (crossed, paired)

        @pl.when(even_strip() == even)
        def _():
            for out, r in ((to_below, 3), (to_above, 0)):
                for f in range(FIELDS):
                    early, late = blocks(f)
                    out[plane + 3 * f, :, :] = early[r : r + 1, :]
                    out[plane + 3 * f + 1, :, :] = early[4 + r : 5 + r, :]
                    out[plane + 3 * f + 2, :, :] = late[r : r + 1, :]


def unpack_rows(paired, crossed, above, below):
    for even in (True, False):

        @pl.when(even_strip() == even)
        def _():
            below[...] = (paired if even else crossed)[...]
            above[...] = (crossed if even else paired)[...]


def edges_kernel(mine, got, cells, paired, crossed):
    for day in (0, 1):

        @pl.when(lax.axis_index("day") == day)
        def _():
            early, late = (mine, got) if day == 0 else (got, mine)
            pack_rows(0, lambda f: (early.at[f], late.at[f]), paired, crossed)

    for even in (True, False):

        @pl.when(even_strip() == even)
        def _():
            paired[9, :, :] = cells[0, 3:4, :] if even else cells[0, 0:1, :]
            crossed[9, :, :] = cells[0, 0:1, :] if even else cells[0, 3:4, :]


def apply_rows(planes, at, terms):
    sums = []
    for c in (0, 1, 2):
        total = planes[M_PLANE + c, :, at] * terms[0]
        total = total + planes[M_PLANE + 3 + c, :, at] * terms[1]
        total = total + planes[M_PLANE + 6 + c, :, at] * terms[2]
        sums.append(total)
    return sums


def apply_columns(planes, at, terms):
    sums = []
    for a in (0, 3, 6):
        total = planes[M_PLANE + a, :, at] * terms[0]
        total = total + planes[M_PLANE + a + 1, :, at] * terms[1]
        total = total + planes[M_PLANE + a + 2, :, at] * terms[2]
        sums.append(total)
    return sums


def inside_kernel(stencil, mine, got, planes, pairs, moved, buffer, semaphores):
    fetch((stencil,), (buffer,), semaphores)
    coefficients(buffer, planes)
    day = lax.axis_index("day")
    tiles = mine.shape[-1] // LANES
    row = position(0) % 4
    first = day == 0
    for f in range(FIELDS + 1):
        for half in (0, 1):
            shifts = (Shift(1), Shift(-1))
            middle = []
            for t in range(tiles + 1):
                if t < tiles:
                    x, y = mine[f, :, tile(t)], got[f, :, tile(t)]
                    u = jnp.where(first, x, y) if half == 0 else jnp.where(first, y, x)
                    pairs[half, f, :, tile(t)] = u
                    if f < FIELDS:
                        up = jnp.where(row == 0, 0.0, rolled(u, 1, 0))
                        down = jnp.where(row == 3, 0.0, rolled(u, -1, 0))
                        left, centre, right = apply_rows(planes, tile(t), (up, u, down))
                        shifts[0].push(left)
                        shifts[1].push(right)
                        middle.append(centre)
                if t >= 1 and f < FIELDS:
                    moved[half, f, :, tile(t - 1)] = middle[t - 1] + shifts[0].take(t - 1) + shifts[1].take(t - 1)


def placed(above, below, index, at):
    row = position(0)
    spread = lambda ref, k: jnp.broadcast_to(ref[k, :, at], (8, LANES))
    first, second = index
    out = jnp.where(row < 2, spread(above, first), spread(below, first))
    if second is not None:
        late = jnp.where(row < 6, spread(above, second), spread(below, second))
        out = jnp.where(row < 4, out, late)
    return out


def total(x):
    return jnp.sum(jnp.sum(x, axis=0, keepdims=True), axis=1, keepdims=True)


def image_kernel(*refs):
    pairs, moved, planes, cells, came_paired, came_crossed = refs[:6]
    image, leaves, rims, gaps, parts, paired, crossed, above, below = refs[6:]
    unpack_rows(came_paired, came_crossed, above, below)
    tiles = moved.shape[-1] // LANES
    row = position(0)
    low = row < 4
    edge = row % 4

    @pl.loop(0, FIELDS)
    def _(f):
        incoming = [(Shift(1), Shift(-1)) for _ in (0, 1)]
        beside = [(Shift(-1), Shift(1)) for _ in (0, 1)]
        kept = {}
        along = square = jnp.zeros((8, LANES), F32)
        for t in range(tiles + 2):
            if t < tiles:
                at = tile(t)
                for half in (0, 1):
                    rim = placed(above, below, (3 * f, 3 * f + 1) if half == 0 else (3 * f + 2, None), at)
                    rims[half, f, :, at] = rim
                    incoming[half][0].push(planes[H_PLANE, :, at] * rim)
                    kept["in", half, t] = planes[H_PLANE + 1, :, at] * rim
                    incoming[half][1].push(planes[H_PLANE + 2, :, at] * rim)
            if 1 <= t <= tiles:
                q = t - 1
                at = tile(q)
                m = [
                    moved[half, f, :, at] + kept.pop(("in", half, q)) + incoming[half][0].take(q) + incoming[half][1].take(q)
                    for half in (0, 1)
                ]
                before = (jnp.where(low, 0.0, rolled(m[0], 4, 0)), rolled(jnp.where(low, m[1], m[0]), 4, 0))
                for half in (0, 1):
                    u = pairs[half, f, :, at]
                    gap = u - before[half]
                    gaps[half, f, :, at] = gap
                    w = cells[1, :, at] * gap
                    beside[half][0].push(w)
                    beside[half][1].push(w)
                    kept[half, q] = (w, w + pairs[half, FIELDS, :, at] * u)
            if t >= 2:
                q = t - 2
                at = tile(q)
                s, out = [], []
                for half in (0, 1):
                    w, kept["own", half] = kept.pop((half, q))
                    up, stay, down = apply_columns(planes, at, (beside[half][0].take(q), w, beside[half][1].take(q)))
                    s.append(stay + jnp.where(edge == 3, 0.0, rolled(up, -1, 0)) + jnp.where(edge == 0, 0.0, rolled(down, 1, 0)))
                    out.append(jnp.where(edge == 0, up, down))
                after = (rolled(jnp.where(low, s[1], s[0]), 4, 0), jnp.where(low, rolled(s[1], 4, 0), 0.0))
                leaves[0, f, :, at] = rolled(jnp.where(low, out[1], out[0]), 4, 0)
                leaves[1, f, :, at] = rolled(out[1], 4, 0)
                for half in (0, 1):
                    z = cells[0, :, at] * (kept.pop(("own", half)) - after[half])
                    image[half, f, :, at] = z
                    u = pairs[half, f, :, at]
                    along = along + u * z
                    square = square + u * u
        parts[0, f, :, :] = along
        parts[1, f, :, :] = square

    pack_rows(0, lambda f: (image.at[0, f], image.at[1, f]), paired, crossed)
    pack_rows(9, lambda f: (leaves.at[0, f], leaves.at[1, f]), paired, crossed)


def centres_kernel(parts, centres):
    for f in range(FIELDS):
        along, square = total(parts[0, f, :, :]), total(parts[1, f, :, :])
        centre = jnp.where(square > 0.0, along / jnp.where(square > 0.0, square, 1.0), 0.0)
        centres[f, :, :] = jnp.broadcast_to(centre, (8, LANES))


def sums_kernel(*refs):
    pairs, part, leaves, gaps, centres, planes, cells = refs[:7]
    first_paired, first_crossed, came_paired, came_crossed = refs[7:11]
    image, rims, swap, sums, sea_above, sea_below, above, below, kept_sums = refs[11:]
    unpack_rows(first_paired.at[9:10], first_crossed.at[9:10], sea_above, sea_below)
    unpack_rows(came_paired, came_crossed, above, below)
    day = lax.axis_index("day")
    tiles = part.shape[-1] // LANES
    row = position(0)
    low = row < 4
    edge = (row % 4 == 0) | (row % 4 == 3)

    @pl.loop(0, FIELDS)
    def _(f):
        shifts = [(Shift(1), Shift(-1)) for _ in (0, 1)]
        kept = {}
        totals = [None] * 6
        ratio = centres[f, :, :]
        for t in range(tiles + 1):
            if t < tiles:
                at = tile(t)
                wet = cells[0, :, at]
                wet_rim = placed(sea_above, sea_below, (0, 0), at)
                for half in (0, 1):
                    days = (3 * f, 3 * f + 1) if half == 0 else (3 * f + 2, None)
                    late = tuple(None if k is None else 9 + k for k in days)
                    came = placed(above, below, late, at)
                    keep = edge if half == 0 else edge & low
                    z = part[half, f, :, at] - jnp.where(keep, wet * came, 0.0)
                    rim = placed(above, below, days, at) - wet_rim * leaves[half, f, :, at]
                    image[half, f, :, at] = z
                    rims[half, f, :, at] = rim
                    up = jnp.where(row % 4 == 0, rim, rolled(z, 1, 0))
                    down = jnp.where(row % 4 == 3, rim, rolled(z, -1, 0))
                    left, centre, right = apply_rows(planes, at, (up, z, down))
                    shifts[half][0].push(left)
                    shifts[half][1].push(right)
                    kept[half, t] = (z, centre)
            if t >= 1:
                q = t - 1
                at = tile(q)
                z, m = [], []
                for half in (0, 1):
                    own, centre = kept.pop((half, q))
                    z.append(own)
                    m.append(centre + shifts[half][0].take(q) + shifts[half][1].take(q))
                before = (jnp.where(low, 0.0, rolled(m[0], 4, 0)), rolled(jnp.where(low, m[1], m[0]), 4, 0))
                terms = [0.0] * 6
                for half in (0, 1):
                    b = pairs[half, f, :, at]
                    y = z[half] - ratio * b
                    seen, gap = pairs[half, FIELDS, :, at], gaps[half, f, :, at]
                    weighted = cells[1, :, at] * gap
                    beside = (z[half] - before[half]) - ratio * gap
                    products = (
                        b * b,
                        b * y,
                        y * y,
                        weighted * gap + seen * b * b,
                        weighted * beside + seen * b * y,
                        cells[1, :, at] * beside * beside + seen * y * y,
                    )
                    terms = [x + product for x, product in zip(terms, products)]
                if q == 0:
                    terms = [jnp.where(day == 0, x, 0.0) for x in terms]
                elif q == tiles - 1:
                    terms = [jnp.where(day == 0, 0.0, x) for x in terms]
                totals = [x if y is None else x + y for x, y in zip(terms, totals)]
        for k, x in enumerate(totals):
            kept_sums[3 * k + f, :, :] = x

    lane = lax.broadcasted_iota(jnp.int32, (1, LANES), 1)
    line = jnp.zeros((1, LANES), F32)
    for k in range(6 * FIELDS):
        line = jnp.where(lane == k, total(kept_sums[k, :, :]), line)
    for f in range(FIELDS):
        line = jnp.where(lane == 6 * FIELDS + f, centres[f, 0:1, :], line)
    for k in range(sums.shape[0]):
        sums[k, :, :] = line
    for which in (0, 1):

        @pl.when(day == which)
        def _():
            for t in range(tiles - 1):
                swap[t, :, :] = image[1 - which, 0, :, tile(t + which)]


def fit_kernel(sums, mine, give, pairs, image, theirs, side_rims, image_rims, posterior, fitted, mean, cells, ready, lines, semaphores):
    day = lax.axis_index("day")
    tiles = mine.shape[-1] // LANES
    row = position(0)
    low = row < 4
    for k in range(sums.shape[0]):
        lines[k : k + 1, :] = sums[k, :, :]
    own = [lines[...]] + [rolled(lines[...], -3 * k, 1) for k in range(1, 7)]
    side_side, side_off, off_off, side_energy, cross_energy, off_energy, centre = own
    add = lambda x: jnp.sum(x, axis=0, keepdims=True)
    norm = add(side_side)
    ratio = add(centre * side_side + side_off) / norm
    move = ratio - centre
    off_norm = add(off_off - 2.0 * move * side_off + move * move * side_side)
    off_energy = add(off_energy - 2.0 * move * cross_energy + move * move * side_energy)
    cross_energy = add(cross_energy - move * side_energy)
    step = 1.0 / ratio
    norm_next = step * step * off_norm
    grown = norm_next / norm
    curvature = step * step * off_energy - 2.0 * step * grown * cross_energy + grown * grown * add(side_energy)
    second = norm_next / curvature
    on_both = (step + second * (1.0 + grown), -second * step)
    weights = [[jnp.broadcast_to(x[:, f : f + 1], (8, LANES)) for x in on_both] for f in range(FIELDS)]

    def store(at, x):
        mean[0, :, at] = x[0:4]
        mean[1, :, at] = x[4:8]

    on_side, on_image = weights[0]
    for which in (0, 1):

        @pl.when(day == which)
        def _():
            for t in range(tiles - 1):
                here, there = which * (tiles - 1), (1 - which) * (tiles - 1)
                own = on_side * mine[0, :, tile(t + which)] + on_image * image[which, 0, :, tile(t + which)]
                store(tile(here + t), own)
                store(tile(there + t), on_side * give[0, :, tile(t + 1 - which)] + on_image * theirs[t, :, :])

    out_mean = pltpu.make_async_copy(mean, posterior, semaphores.at[0])
    out_mean.start()

    wide = {(f, half): (Shift(1), Shift(-1)) for f in (1, 2) for half in (0, 1)}
    kept = {}
    for t in range(tiles + 1):
        if t < tiles:
            at = tile(t)
            for f in (1, 2):
                on_side, on_image = weights[f]
                for half in (0, 1):
                    x = on_side * pairs[half, f, :, at] + on_image * image[half, f, :, at]
                    rim = on_side * side_rims[half, f, :, at] + on_image * image_rims[half, f, :, at]
                    up = jnp.where(row % 4 == 0, rim, rolled(x, 1, 0))
                    down = jnp.where(row % 4 == 3, rim, rolled(x, -1, 0))
                    box = x + up + down
                    wide[f, half][0].push(box)
                    wide[f, half][1].push(box)
                    kept[f, half, t] = (x, box)
        if t >= 1:
            q = t - 1
            totals = [0.0] * 5
            for f in (1, 2):
                (x0, box0), (x1, box1) = kept.pop((f, 0, q)), kept.pop((f, 1, q))
                targets = (rolled(jnp.where(low, x1, x0), 4, 0), rolled(x1, 4, 0))
                for half, (x, box) in enumerate(((x0, box0), (x1, box1))):
                    lap = box + wide[f, half][0].take(q) + wide[f, half][1].take(q) - 9.0 * x
                    if half == 1:
                        x, lap = jnp.where(low, x, 0.0), jnp.where(low, lap, 0.0)
                    target = targets[half]
                    for k, term in enumerate((x * x, x * lap, lap * lap, x * target, lap * target)):
                        totals[k] = totals[k] + term
            m = [x + rolled(x, 4, 0) for x in totals]
            first, second = m[0] + RIDGE, m[2] + RIDGE
            inverse = 1.0 / (first * second - m[1] * m[1])
            persistence = (second * m[3] - m[1] * m[4]) * inverse
            diffusion = (first * m[4] - m[1] * m[3]) * inverse

            cells[0, :, tile(q)] = persistence[0:4]
            cells[1, :, tile(q)] = diffusion[0:4]
    for which in (0, 1):

        @pl.when(day == which)
        def _():
            ready[...] = cells[:, :, which * LANES : which * LANES + ready.shape[-1]]

    out_fit = pltpu.make_async_copy(ready, fitted, semaphores.at[1])
    out_fit.start()
    out_mean.wait()
    out_fit.wait()


VMEM = pl.BlockSpec(memory_space=pltpu.VMEM)
HBM = pl.BlockSpec(memory_space=pltpu.HBM)


def call(kernel, outs, *args, scratch=(), source=None, target=VMEM, flops=2_000_000):
    size = sum(x.size * x.dtype.itemsize for x in args)
    return pl.pallas_call(
        kernel,
        out_shape=[jax.ShapeDtypeStruct(shape, F32) for shape in outs],
        in_specs=source or [VMEM] * len(args),
        out_specs=[target] * len(outs),
        scratch_shapes=scratch,
        cost_estimate=pl.CostEstimate(flops=flops, bytes_accessed=size, transcendentals=0),
        compiler_params=pltpu.CompilerParams(vmem_limit_bytes=32 << 20),
    )(*args)


def kept_in_hbm(*args):
    return tuple(pltpu.with_memory_space_constraint(x, pltpu.HBM) for x in args)


def buffers(*args):
    return [pltpu.VMEM(x.shape, x.dtype) for x in args] + [pltpu.SemaphoreType.DMA((len(args),))]


def shards(observed, gap_mask, sea_mask, stencil, precision, noise_precision, perturbation):
    cols = observed.shape[-1]
    devices = lax.axis_size("space") * lax.axis_size("day")
    half = cols // 2
    width = half + LANES
    pair = (8, width)
    row = (1, width)
    same = lambda s: s
    paired_space = lambda s: s ^ 1
    crossed_space = lambda s: ((s + 1) ^ 1) - 1

    raw = kept_in_hbm(observed, gap_mask, sea_mask, precision, noise_precision, perturbation)
    mine, give, cells = call(
        right_sides_kernel, [(4, *pair)] * 2 + [(2, *pair)], *raw, scratch=buffers(*raw), source=[HBM] * len(raw)
    )
    got = send(give, same, lambda d: 1 - d)
    paired, crossed = call(edges_kernel, [(10, *row)] * 2, mine, got, cells)
    first_paired = send(paired, paired_space)
    first_crossed = send(crossed, crossed_space)
    raw = kept_in_hbm(stencil)
    planes, pairs, moved = call(
        inside_kernel,
        [(PLANES, *pair), (2, 4, *pair), (2, 3, *pair)],
        *raw, mine, got,
        scratch=buffers(*raw),
        source=[HBM, VMEM, VMEM],
    )
    part, leaves, side_rims, gaps, parts, paired, crossed = call(
        image_kernel,
        [(2, 3, *pair)] * 4 + [(2, FIELDS, 8, LANES)] + [(18, *row)] * 2,
        pairs, moved, planes, cells, first_paired, first_crossed,
        scratch=[pltpu.VMEM((10, *row), F32)] * 2,
    )
    paired = send(paired, paired_space)
    crossed = send(crossed, crossed_space)
    (centres,) = call(centres_kernel, [(FIELDS, 8, LANES)], parts)
    image, image_rims, swap, sums = call(
        sums_kernel,
        [(2, 3, *pair), (2, 3, *pair), (half // LANES, 8, LANES), (devices, 1, LANES)],
        pairs, part, leaves, gaps, centres, planes, cells, first_paired, first_crossed, paired, crossed,
        scratch=[pltpu.VMEM((1, *row), F32)] * 2 + [pltpu.VMEM((18, *row), F32)] * 2 + [pltpu.VMEM((6 * FIELDS, 8, LANES), F32)],
    )
    theirs = send(swap, same, lambda d: 1 - d)
    sums = lax.all_to_all(sums, ("space", "day"), 0, 0)
    fit = (2, observed.shape[1])
    posterior, fitted = call(
        fit_kernel,
        [observed.shape, (*fit, half)],
        sums, mine, give, pairs, image, theirs, side_rims, image_rims,
        scratch=[
            pltpu.VMEM(observed.shape, F32),
            pltpu.VMEM((*fit, width), F32),
            pltpu.VMEM((*fit, half), F32),
            pltpu.VMEM((devices, LANES), F32),
            pltpu.SemaphoreType.DMA((2,)),
        ],
        target=HBM,
    )
    return posterior, fitted


def solution(mesh):
    placed_args = (
        P("day", ("region", "space"), None),
        P("day", ("region", "space"), None),
        P(("region", "space"), None),
        P(None, ("region", "space"), None),
        P(("region", "space"), None),
        P(("region", "space"), None),
        P(None, "day", ("region", "space"), None),
    )
    return jax.shard_map(
        shards,
        mesh=mesh,
        in_specs=placed_args,
        out_specs=(P("day", ("region", "space"), None), P(None, ("region", "space"), "day")),
        check_vma=False,
    )
```

```python
import jax
import jax.numpy as jnp
from jax import lax
from jax.experimental import pallas as pl
from jax.experimental.pallas import tpu as pltpu
from jax.sharding import PartitionSpec as P

RIDGE = 1.0
LANES = 128
FIELDS = 3
F32 = jnp.float32

M_PLANE, H_PLANE, PLANES = 0, 9, 12


def send(x, space_of, day_of=lambda d: d):
    spaces, days = lax.axis_size("space"), lax.axis_size("day")
    pairs = []
    for s in range(spaces):
        for d in range(days):
            to_s, to_d = space_of(s), day_of(d)
            if 0 <= to_s < spaces:
                pairs.append((s * days + d, to_s * days + to_d))
    return lax.ppermute(x, ("space", "day"), pairs)


def position(axis):
    return lax.broadcasted_iota(jnp.int32, (8, LANES), axis)


def rolled(x, step, axis):
    return pltpu.roll(x, step % x.shape[axis], axis)


def tile(t):
    return pl.ds(t * LANES, LANES)


def dynamic_tile(start, t):
    return pl.ds(pl.multiple_of(start + t * LANES, LANES), LANES)


def doubled(x):
    return jnp.concatenate([x, x], 0)


class Shift:
    def __init__(self, step):
        self.step, self.edge, self.tiles = step, (0 if step > 0 else LANES - 1), []

    def push(self, x):
        self.tiles.append(rolled(x, self.step, 1))

    def take(self, t):
        beside = t - self.step
        here = self.tiles[t]
        other = self.tiles[beside] if 0 <= beside < len(self.tiles) else jnp.zeros_like(here)
        return jnp.where(position(1) == self.edge, other, here)


def fetch(sources, buffers, semaphores):
    copies = [pltpu.make_async_copy(x, y, semaphores.at[k]) for k, (x, y) in enumerate(zip(sources, buffers))]
    for copy in copies:
        copy.start()
    for copy in copies:
        copy.wait()


def right_sides_kernel(*refs):
    sources, (mine, give, cells), buffers, semaphores = refs[:6], refs[6:9], refs[9:15], refs[15]
    fetch(sources, buffers, semaphores)
    observed, gap, sea, precision, noise, perturbation = buffers
    day = lax.axis_index("day")
    tiles = mine.shape[-1] // LANES
    reach = observed.shape[-1] - mine.shape[-1]
    for out, side in ((mine, day), (give, 1 - day)):
        start = side * reach
        for t in range(tiles):
            at = dynamic_tile(start, t)
            both = lambda ref, *lead: jnp.concatenate([ref[(*lead, 0, slice(None), at)], ref[(*lead, 1, slice(None), at)]], 0)
            wet = doubled(sea[:, at].astype(F32))
            if out is mine:
                cells[0, :, tile(t)] = wet
                cells[1, :, tile(t)] = doubled(precision[:, at])
            seen = doubled(noise[:, at]) * both(gap).astype(F32)
            base = wet * seen * both(observed)
            spread = wet * jnp.sqrt(doubled(precision[:, at]) + seen)
            out[0, :, tile(t)] = base
            out[1, :, tile(t)] = base + spread * both(perturbation, 0).astype(F32)
            out[2, :, tile(t)] = base + spread * both(perturbation, 1).astype(F32)
            out[3, :, tile(t)] = seen


def coefficients(stencil, planes):
    width = planes.shape[-1]
    tiles = width // LANES
    start = lax.axis_index("day") * (stencil.shape[-1] - width)
    row = position(0) % 4
    shifts = {(a, c): Shift(c) for a in (-1, 0, 1) for c in (-1, 1)}
    middle = {}
    for t in range(tiles + 1):
        if t < tiles:
            at = dynamic_tile(start, t)
            for a in (-1, 0, 1):
                for c in (-1, 0, 1):
                    s = doubled(stencil[3 * (a + 1) + c + 1, :, at].astype(F32))
                    if c == 0:
                        middle[a, t] = s
                    else:
                        shifts[a, c].push(s)
        if t >= 1:
            for c in (-1, 0, 1):
                got = {a: shifts[a, c].take(t - 1) if c else middle.pop((a, t - 1)) for a in (-1, 0, 1)}
                for a in (-1, 0, 1):
                    planes[M_PLANE + 3 * (a + 1) + c + 1, :, tile(t - 1)] = got[a]
                planes[H_PLANE + c + 1, :, tile(t - 1)] = jnp.where(row == 0, got[-1], jnp.where(row == 3, got[1], 0.0))


def even_strip():
    return lax.axis_index("space") % 2 == 0


def pack_rows(plane, blocks, paired, crossed):
    for even in (True, False):
        to_below, to_above = (paired, crossed) if even else (crossed, paired)

        @pl.when(even_strip() == even)
        def _():
            for out, r in ((to_below, 3), (to_above, 0)):
                for f in range(FIELDS):
                    early, late = blocks(f)
                    out[plane + 3 * f, :, :] = early[r : r + 1, :]
                    out[plane + 3 * f + 1, :, :] = early[4 + r : 5 + r, :]
                    out[plane + 3 * f + 2, :, :] = late[r : r + 1, :]


def unpack_rows(paired, crossed, above, below):
    for even in (True, False):

        @pl.when(even_strip() == even)
        def _():
            below[...] = (paired if even else crossed)[...]
            above[...] = (crossed if even else paired)[...]


def edges_kernel(mine, got, cells, paired, crossed):
    for day in (0, 1):

        @pl.when(lax.axis_index("day") == day)
        def _():
            early, late = (mine, got) if day == 0 else (got, mine)
            pack_rows(0, lambda f: (early.at[f], late.at[f]), paired, crossed)

    for even in (True, False):

        @pl.when(even_strip() == even)
        def _():
            paired[9, :, :] = cells[0, 3:4, :] if even else cells[0, 0:1, :]
            crossed[9, :, :] = cells[0, 0:1, :] if even else cells[0, 3:4, :]


def apply_rows(planes, at, terms):
    sums = []
    for c in (0, 1, 2):
        total = planes[M_PLANE + c, :, at] * terms[0]
        total = total + planes[M_PLANE + 3 + c, :, at] * terms[1]
        total = total + planes[M_PLANE + 6 + c, :, at] * terms[2]
        sums.append(total)
    return sums


def apply_columns(planes, at, terms):
    sums = []
    for a in (0, 3, 6):
        total = planes[M_PLANE + a, :, at] * terms[0]
        total = total + planes[M_PLANE + a + 1, :, at] * terms[1]
        total = total + planes[M_PLANE + a + 2, :, at] * terms[2]
        sums.append(total)
    return sums


def inside_kernel(stencil, mine, got, planes, pairs, moved, buffer, semaphores):
    fetch((stencil,), (buffer,), semaphores)
    coefficients(buffer, planes)
    day = lax.axis_index("day")
    tiles = mine.shape[-1] // LANES
    row = position(0) % 4
    first = day == 0
    for f in range(FIELDS + 1):
        for half in (0, 1):
            shifts = (Shift(1), Shift(-1))
            middle = []
            for t in range(tiles + 1):
                if t < tiles:
                    x, y = mine[f, :, tile(t)], got[f, :, tile(t)]
                    u = jnp.where(first, x, y) if half == 0 else jnp.where(first, y, x)
                    pairs[half, f, :, tile(t)] = u
                    if f < FIELDS:
                        up = jnp.where(row == 0, 0.0, rolled(u, 1, 0))
                        down = jnp.where(row == 3, 0.0, rolled(u, -1, 0))
                        left, centre, right = apply_rows(planes, tile(t), (up, u, down))
                        shifts[0].push(left)
                        shifts[1].push(right)
                        middle.append(centre)
                if t >= 1 and f < FIELDS:
                    moved[half, f, :, tile(t - 1)] = middle[t - 1] + shifts[0].take(t - 1) + shifts[1].take(t - 1)


def placed(above, below, index, at):
    row = position(0)
    spread = lambda ref, k: jnp.broadcast_to(ref[k, :, at], (8, LANES))
    first, second = index
    out = jnp.where(row < 2, spread(above, first), spread(below, first))
    if second is not None:
        late = jnp.where(row < 6, spread(above, second), spread(below, second))
        out = jnp.where(row < 4, out, late)
    return out


def total(x):
    return jnp.sum(jnp.sum(x, axis=0, keepdims=True), axis=1, keepdims=True)


def image_kernel(*refs):
    pairs, moved, planes, cells, came_paired, came_crossed = refs[:6]
    image, leaves, rims, gaps, parts, paired, crossed, above, below = refs[6:]
    unpack_rows(came_paired, came_crossed, above, below)
    tiles = moved.shape[-1] // LANES
    row = position(0)
    low = row < 4
    edge = row % 4

    @pl.loop(0, FIELDS)
    def _(f):
        incoming = [(Shift(1), Shift(-1)) for _ in (0, 1)]
        beside = [(Shift(-1), Shift(1)) for _ in (0, 1)]
        kept = {}
        along = square = jnp.zeros((8, LANES), F32)
        for t in range(tiles + 2):
            if t < tiles:
                at = tile(t)
                for half in (0, 1):
                    rim = placed(above, below, (3 * f, 3 * f + 1) if half == 0 else (3 * f + 2, None), at)
                    rims[half, f, :, at] = rim
                    incoming[half][0].push(planes[H_PLANE, :, at] * rim)
                    kept["in", half, t] = planes[H_PLANE + 1, :, at] * rim
                    incoming[half][1].push(planes[H_PLANE + 2, :, at] * rim)
            if 1 <= t <= tiles:
                q = t - 1
                at = tile(q)
                m = [
                    moved[half, f, :, at] + kept.pop(("in", half, q)) + incoming[half][0].take(q) + incoming[half][1].take(q)
                    for half in (0, 1)
                ]
                before = (jnp.where(low, 0.0, rolled(m[0], 4, 0)), rolled(jnp.where(low, m[1], m[0]), 4, 0))
                for half in (0, 1):
                    u = pairs[half, f, :, at]
                    gap = u - before[half]
                    gaps[half, f, :, at] = gap
                    w = cells[1, :, at] * gap
                    beside[half][0].push(w)
                    beside[half][1].push(w)
                    kept[half, q] = (w, w + pairs[half, FIELDS, :, at] * u)
            if t >= 2:
                q = t - 2
                at = tile(q)
                s, out = [], []
                for half in (0, 1):
                    w, kept["own", half] = kept.pop((half, q))
                    up, stay, down = apply_columns(planes, at, (beside[half][0].take(q), w, beside[half][1].take(q)))
                    s.append(stay + jnp.where(edge == 3, 0.0, rolled(up, -1, 0)) + jnp.where(edge == 0, 0.0, rolled(down, 1, 0)))
                    out.append(jnp.where(edge == 0, up, down))
                after = (rolled(jnp.where(low, s[1], s[0]), 4, 0), jnp.where(low, rolled(s[1], 4, 0), 0.0))
                leaves[0, f, :, at] = rolled(jnp.where(low, out[1], out[0]), 4, 0)
                leaves[1, f, :, at] = rolled(out[1], 4, 0)
                for half in (0, 1):
                    z = cells[0, :, at] * (kept.pop(("own", half)) - after[half])
                    image[half, f, :, at] = z
                    u = pairs[half, f, :, at]
                    along = along + u * z
                    square = square + u * u
        parts[0, f, :, :] = along
        parts[1, f, :, :] = square

    pack_rows(0, lambda f: (image.at[0, f], image.at[1, f]), paired, crossed)
    pack_rows(9, lambda f: (leaves.at[0, f], leaves.at[1, f]), paired, crossed)


def centres_kernel(parts, centres):
    for f in range(FIELDS):
        along, square = total(parts[0, f, :, :]), total(parts[1, f, :, :])
        centre = jnp.where(square > 0.0, along / jnp.where(square > 0.0, square, 1.0), 0.0)
        centres[f, :, :] = jnp.broadcast_to(centre, (8, LANES))


def sums_kernel(*refs):
    pairs, part, leaves, gaps, centres, planes, cells = refs[:7]
    first_paired, first_crossed, came_paired, came_crossed = refs[7:11]
    image, rims, swap, sums, sea_above, sea_below, above, below, kept_sums = refs[11:]
    unpack_rows(first_paired.at[9:10], first_crossed.at[9:10], sea_above, sea_below)
    unpack_rows(came_paired, came_crossed, above, below)
    day = lax.axis_index("day")
    tiles = part.shape[-1] // LANES
    row = position(0)
    low = row < 4
    edge = (row % 4 == 0) | (row % 4 == 3)

    @pl.loop(0, FIELDS)
    def _(f):
        shifts = [(Shift(1), Shift(-1)) for _ in (0, 1)]
        kept = {}
        totals = [None] * 6
        ratio = centres[f, :, :]
        for t in range(tiles + 1):
            if t < tiles:
                at = tile(t)
                wet = cells[0, :, at]
                wet_rim = placed(sea_above, sea_below, (0, 0), at)
                for half in (0, 1):
                    days = (3 * f, 3 * f + 1) if half == 0 else (3 * f + 2, None)
                    late = tuple(None if k is None else 9 + k for k in days)
                    came = placed(above, below, late, at)
                    keep = edge if half == 0 else edge & low
                    z = part[half, f, :, at] - jnp.where(keep, wet * came, 0.0)
                    rim = placed(above, below, days, at) - wet_rim * leaves[half, f, :, at]
                    image[half, f, :, at] = z
                    rims[half, f, :, at] = rim
                    up = jnp.where(row % 4 == 0, rim, rolled(z, 1, 0))
                    down = jnp.where(row % 4 == 3, rim, rolled(z, -1, 0))
                    left, centre, right = apply_rows(planes, at, (up, z, down))
                    shifts[half][0].push(left)
                    shifts[half][1].push(right)
                    kept[half, t] = (z, centre)
            if t >= 1:
                q = t - 1
                at = tile(q)
                z, m = [], []
                for half in (0, 1):
                    own, centre = kept.pop((half, q))
                    z.append(own)
                    m.append(centre + shifts[half][0].take(q) + shifts[half][1].take(q))
                before = (jnp.where(low, 0.0, rolled(m[0], 4, 0)), rolled(jnp.where(low, m[1], m[0]), 4, 0))
                terms = [0.0] * 6
                for half in (0, 1):
                    b = pairs[half, f, :, at]
                    y = z[half] - ratio * b
                    seen, gap = pairs[half, FIELDS, :, at], gaps[half, f, :, at]
                    weighted = cells[1, :, at] * gap
                    beside = (z[half] - before[half]) - ratio * gap
                    products = (
                        b * b,
                        b * y,
                        y * y,
                        weighted * gap + seen * b * b,
                        weighted * beside + seen * b * y,
                        cells[1, :, at] * beside * beside + seen * y * y,
                    )
                    terms = [x + product for x, product in zip(terms, products)]
                if q == 0:
                    terms = [jnp.where(day == 0, x, 0.0) for x in terms]
                elif q == tiles - 1:
                    terms = [jnp.where(day == 0, 0.0, x) for x in terms]
                totals = [x if y is None else x + y for x, y in zip(terms, totals)]
        for k, x in enumerate(totals):
            kept_sums[3 * k + f, :, :] = x

    lane = lax.broadcasted_iota(jnp.int32, (1, LANES), 1)
    line = jnp.zeros((1, LANES), F32)
    for k in range(6 * FIELDS):
        line = jnp.where(lane == k, total(kept_sums[k, :, :]), line)
    for f in range(FIELDS):
        line = jnp.where(lane == 6 * FIELDS + f, centres[f, 0:1, :], line)
    for k in range(sums.shape[0]):
        sums[k, :, :] = line
    for which in (0, 1):

        @pl.when(day == which)
        def _():
            for t in range(tiles - 1):
                swap[t, :, :] = image[1 - which, 0, :, tile(t + which)]


def fit_kernel(sums, mine, give, pairs, image, theirs, side_rims, image_rims, posterior, fitted, mean, cells, lines, semaphores):
    day = lax.axis_index("day")
    tiles = mine.shape[-1] // LANES
    row = position(0)
    low = row < 4
    for k in range(sums.shape[0]):
        lines[k : k + 1, :] = sums[k, :, :]
    own = [lines[...]] + [rolled(lines[...], -3 * k, 1) for k in range(1, 7)]
    side_side, side_off, off_off, side_energy, cross_energy, off_energy, centre = own
    add = lambda x: jnp.sum(x, axis=0, keepdims=True)
    norm = add(side_side)
    ratio = add(centre * side_side + side_off) / norm
    move = ratio - centre
    off_norm = add(off_off - 2.0 * move * side_off + move * move * side_side)
    off_energy = add(off_energy - 2.0 * move * cross_energy + move * move * side_energy)
    cross_energy = add(cross_energy - move * side_energy)
    step = 1.0 / ratio
    norm_next = step * step * off_norm
    grown = norm_next / norm
    curvature = step * step * off_energy - 2.0 * step * grown * cross_energy + grown * grown * add(side_energy)
    second = norm_next / curvature
    on_both = (step + second * (1.0 + grown), -second * step)
    weights = [[jnp.broadcast_to(x[:, f : f + 1], (8, LANES)) for x in on_both] for f in range(FIELDS)]

    def store(at, x):
        mean[0, :, at] = x[0:4]
        mean[1, :, at] = x[4:8]

    on_side, on_image = weights[0]
    for which in (0, 1):

        @pl.when(day == which)
        def _():
            for t in range(tiles - 1):
                here, there = which * (tiles - 1), (1 - which) * (tiles - 1)
                own = on_side * mine[0, :, tile(t + which)] + on_image * image[which, 0, :, tile(t + which)]
                store(tile(here + t), own)
                store(tile(there + t), on_side * give[0, :, tile(t + 1 - which)] + on_image * theirs[t, :, :])

    out_mean = pltpu.make_async_copy(mean, posterior, semaphores.at[0])
    out_mean.start()
    middle = (tiles - 1) // 2
    part = middle * LANES

    def fit_copy(k):
        source = pl.ds(pl.multiple_of(day * LANES + k * part, LANES), part)
        return pltpu.make_async_copy(cells.at[:, :, source], fitted.at[:, :, k * part : (k + 1) * part], semaphores.at[1 + k])

    out_fit = [fit_copy(0), fit_copy(1)]

    wide = {(f, half): (Shift(1), Shift(-1)) for f in (1, 2) for half in (0, 1)}
    kept = {}
    for t in range(tiles + 1):
        if t < tiles:
            at = tile(t)
            for f in (1, 2):
                on_side, on_image = weights[f]
                for half in (0, 1):
                    x = on_side * pairs[half, f, :, at] + on_image * image[half, f, :, at]
                    rim = on_side * side_rims[half, f, :, at] + on_image * image_rims[half, f, :, at]
                    up = jnp.where(row % 4 == 0, rim, rolled(x, 1, 0))
                    down = jnp.where(row % 4 == 3, rim, rolled(x, -1, 0))
                    box = x + up + down
                    wide[f, half][0].push(box)
                    wide[f, half][1].push(box)
                    kept[f, half, t] = (x, box)
        if t >= 1:
            q = t - 1
            totals = [0.0] * 5
            for f in (1, 2):
                (x0, box0), (x1, box1) = kept.pop((f, 0, q)), kept.pop((f, 1, q))
                targets = (rolled(jnp.where(low, x1, x0), 4, 0), rolled(x1, 4, 0))
                for half, (x, box) in enumerate(((x0, box0), (x1, box1))):
                    lap = box + wide[f, half][0].take(q) + wide[f, half][1].take(q) - 9.0 * x
                    if half == 1:
                        x, lap = jnp.where(low, x, 0.0), jnp.where(low, lap, 0.0)
                    target = targets[half]
                    for k, term in enumerate((x * x, x * lap, lap * lap, x * target, lap * target)):
                        totals[k] = totals[k] + term
            m = [x + rolled(x, 4, 0) for x in totals]
            first, second = m[0] + RIDGE, m[2] + RIDGE
            inverse = 1.0 / (first * second - m[1] * m[1])
            persistence = (second * m[3] - m[1] * m[4]) * inverse
            diffusion = (first * m[4] - m[1] * m[3]) * inverse

            cells[0, :, tile(q)] = persistence[0:4]
            cells[1, :, tile(q)] = diffusion[0:4]
            if q == middle:
                out_fit[0].start()
    out_fit[1].start()
    out_mean.wait()
    for copy in out_fit:
        copy.wait()


VMEM = pl.BlockSpec(memory_space=pltpu.VMEM)
HBM = pl.BlockSpec(memory_space=pltpu.HBM)


def call(kernel, outs, *args, scratch=(), source=None, target=VMEM, flops=2_000_000):
    size = sum(x.size * x.dtype.itemsize for x in args)
    return pl.pallas_call(
        kernel,
        out_shape=[jax.ShapeDtypeStruct(shape, F32) for shape in outs],
        in_specs=source or [VMEM] * len(args),
        out_specs=[target] * len(outs),
        scratch_shapes=scratch,
        cost_estimate=pl.CostEstimate(flops=flops, bytes_accessed=size, transcendentals=0),
        compiler_params=pltpu.CompilerParams(vmem_limit_bytes=32 << 20),
    )(*args)


def kept_in_hbm(*args):
    return tuple(pltpu.with_memory_space_constraint(x, pltpu.HBM) for x in args)


def buffers(*args):
    return [pltpu.VMEM(x.shape, x.dtype) for x in args] + [pltpu.SemaphoreType.DMA((len(args),))]


def shards(observed, gap_mask, sea_mask, stencil, precision, noise_precision, perturbation):
    cols = observed.shape[-1]
    devices = lax.axis_size("space") * lax.axis_size("day")
    half = cols // 2
    width = half + LANES
    pair = (8, width)
    row = (1, width)
    same = lambda s: s
    paired_space = lambda s: s ^ 1
    crossed_space = lambda s: ((s + 1) ^ 1) - 1

    raw = kept_in_hbm(observed, gap_mask, sea_mask, precision, noise_precision, perturbation)
    mine, give, cells = call(
        right_sides_kernel, [(4, *pair)] * 2 + [(2, *pair)], *raw, scratch=buffers(*raw), source=[HBM] * len(raw)
    )
    got = send(give, same, lambda d: 1 - d)
    paired, crossed = call(edges_kernel, [(10, *row)] * 2, mine, got, cells)
    first_paired = send(paired, paired_space)
    first_crossed = send(crossed, crossed_space)
    raw = kept_in_hbm(stencil)
    planes, pairs, moved = call(
        inside_kernel,
        [(PLANES, *pair), (2, 4, *pair), (2, 3, *pair)],
        *raw, mine, got,
        scratch=buffers(*raw),
        source=[HBM, VMEM, VMEM],
    )
    part, leaves, side_rims, gaps, parts, paired, crossed = call(
        image_kernel,
        [(2, 3, *pair)] * 4 + [(2, FIELDS, 8, LANES)] + [(18, *row)] * 2,
        pairs, moved, planes, cells, first_paired, first_crossed,
        scratch=[pltpu.VMEM((10, *row), F32)] * 2,
    )
    paired = send(paired, paired_space)
    crossed = send(crossed, crossed_space)
    (centres,) = call(centres_kernel, [(FIELDS, 8, LANES)], parts)
    image, image_rims, swap, sums = call(
        sums_kernel,
        [(2, 3, *pair), (2, 3, *pair), (half // LANES, 8, LANES), (devices, 1, LANES)],
        pairs, part, leaves, gaps, centres, planes, cells, first_paired, first_crossed, paired, crossed,
        scratch=[pltpu.VMEM((1, *row), F32)] * 2 + [pltpu.VMEM((18, *row), F32)] * 2 + [pltpu.VMEM((6 * FIELDS, 8, LANES), F32)],
    )
    theirs = send(swap, same, lambda d: 1 - d)
    sums = lax.all_to_all(sums, ("space", "day"), 0, 0)
    fit = (2, observed.shape[1])
    posterior, fitted = call(
        fit_kernel,
        [observed.shape, (*fit, half)],
        sums, mine, give, pairs, image, theirs, side_rims, image_rims,
        scratch=[
            pltpu.VMEM(observed.shape, F32),
            pltpu.VMEM((*fit, width), F32),
            pltpu.VMEM((devices, LANES), F32),
            pltpu.SemaphoreType.DMA((3,)),
        ],
        target=HBM,
    )
    return posterior, fitted


def solution(mesh):
    placed_args = (
        P("day", ("region", "space"), None),
        P("day", ("region", "space"), None),
        P(("region", "space"), None),
        P(None, ("region", "space"), None),
        P(("region", "space"), None),
        P(("region", "space"), None),
        P(None, "day", ("region", "space"), None),
    )
    return jax.shard_map(
        shards,
        mesh=mesh,
        in_specs=placed_args,
        out_specs=(P("day", ("region", "space"), None), P(None, ("region", "space"), "day")),
        check_vma=False,
    )
```
